32 devices in a mesh: row: 4 (over x, core), col: 8 (over z, y).
Axes of the slice: x: 2, y: 2, z: 4, core: 2. Of those that a mesh axis runs over, the one named last changes fastest.
Arguments:
- integrals: bfloat16 [384, 64, 4096], P(('row', 'col')), may hold values from -6 to 6
- block_list: int32 [384, 3], P(('row', 'col')), may hold values from 0 to 31, as said below
- p_slot: int32 [16], replicated, may hold values from 0 to 15, as said below
- metric: bfloat16 [16, 64, 64], P('col'), may hold values from -0.75 to 0.75
- density_panel: bfloat16 [2048, 128], P(('row', 'col')), may hold values from -0.75 to 0.75
- pattern: int32 [2048], P(('row', 'col')), may hold values 0 or 1
Outputs:
- exchange_blocks: float32 [2048, 512], P(('row', 'col'))
The draws below stay inside these ranges and needn't reach their ends.
Inputs may be any that keep to these rules, and one draw needn't show every extreme that they name: `block_list`: rows name (mu block, nu block, auxiliary block). The 12 rows of the device at position row * 8 + col have mu blocks in row * 8 to row * 8 + 7. With owner p_slot[p] // 2, no device lists more than 2 blocks for one owner, and in every row group some owner gets exactly 2 from every device of the group. A permutation; auxiliary block p is contracted by col index p_slot[p] // 2, local slot p_slot[p] % 2.
All inputs are finite; a program needn't handle non-finite values. No bound on the sum of `pattern` on one device may be relied on, other than what follows from the above.
Results may differ from the reference program's by a relative error of at most 0.00059.
Values may be sent and summed in bfloat16 or wider, within the bound.
A program may use at most 192 MiB of HBM per device.

```python
import jax
import jax.numpy as jnp
from jax import lax

BS = 64
MB = 8
PB = 2
OCC = 128
E_DEV = 12
NBLK = 32
NPB = 16
ORBS = 2048
BLOCKS = 384
N_ROW = 4
N_COL = 8


def slot_order(key):
    return jax.random.permutation(jax.random.fold_in(key, 11), NPB).astype(jnp.int32)


def draw_p_slot(key, part):
    return slot_order(key)


def draw_block_list(key, part):
    ordering = slot_order(key)
    inverse = jnp.argsort(ordering, stable=True).astype(jnp.int32)
    devices = N_ROW * N_COL
    draw_key = jax.random.fold_in(key, 23)
    row_of_device = jnp.arange(devices, dtype=jnp.int32) // N_COL
    favored = jax.random.randint(jax.random.fold_in(draw_key, 1), (N_ROW,), 0, N_COL).astype(jnp.int32)
    device_keys = jax.random.split(jax.random.fold_in(draw_key, 2), devices)
    orders = jax.vmap(lambda k: jax.random.permutation(k, N_COL))(device_keys).astype(jnp.int32)
    starred = favored[row_of_device]
    star_place = jnp.argmax(orders == starred[:, None], axis=1)
    leading = orders[:, 0]
    positions = jnp.arange(N_COL, dtype=jnp.int32)[None, :]
    orders = jnp.where(positions == star_place[:, None], leading[:, None], orders)
    orders = jnp.where(positions == 0, starred[:, None], orders)
    pick_index = jnp.arange(E_DEV, dtype=jnp.int32) % N_COL
    owners = orders[:, pick_index]
    local_slot = jax.random.randint(jax.random.fold_in(draw_key, 3), (devices, E_DEV), 0, PB).astype(jnp.int32)
    fitting = inverse[owners * PB + local_slot]
    first_blocks = row_of_device[:, None] * MB + jax.random.randint(jax.random.fold_in(draw_key, 4), (devices, E_DEV), 0, MB).astype(jnp.int32)
    second_blocks = jax.random.randint(jax.random.fold_in(draw_key, 5), (devices, E_DEV), 0, NBLK).astype(jnp.int32)
    return jnp.stack([first_blocks, second_blocks, fitting], axis=-1).reshape(devices * E_DEV, 3).astype(jnp.int32)


def with_ends(array, rng, low, largest):
    longest = array.shape.index(max(array.shape))
    spots = []
    for shift in (0, 1):
        where = [jax.random.randint(jax.random.fold_in(rng, axis), (), 0, length) for axis, length in enumerate(array.shape)]
        where[longest] = (where[longest] + shift) % array.shape[longest]
        spots.append(tuple(where))
    return array.at[spots[0]].set(low).at[spots[1]].set(largest)


def levels(key, extent, shards, low, high):
    loudness, own = 1.0, jax.random.fold_in(key, 6)
    for axis_at, shards_of in shards:
        steps = jnp.exp(jax.random.uniform(jax.random.fold_in(own, axis_at), (shards_of,), jnp.float32, low / len(shards), high / len(shards)))
        loudness = loudness * jnp.repeat(steps, extent[axis_at] // shards_of).reshape([-1 if axis == axis_at else 1 for axis in range(len(extent))])
    return loudness


def scatter_about(own_key, extent, spread, limit, pieces=(), kind=jnp.bfloat16):
    array = spread * jax.random.normal(own_key, extent, jnp.float32)
    if pieces:
        array = array * levels(own_key, extent, pieces, -0.22, 0.18)
    return jnp.clip(array, -limit, limit).astype(kind)


def setup_inputs(seed: int = 0) -> dict:
    splits = jax.random.split(jax.random.key(seed), 7)
    return {
        "integrals": scatter_about(splits[0], (BLOCKS, BS, BS * BS), 1.0, 6.0, ((0, 32),)),
        "block_list": draw_block_list(jax.random.fold_in(splits[6], 71), 0),
        "p_slot": draw_p_slot(jax.random.fold_in(splits[6], 71), 0),
        "metric": scatter_about(splits[3], (NPB, BS, BS), BS ** -0.5, 0.75, ((0, 8),)),
        "density_panel": scatter_about(splits[4], (ORBS, OCC), BS ** -0.5, 0.75, ((0, 32),)),
        "pattern": with_ends((jax.random.randint(splits[5], (ORBS,), 0, 4) < 3).astype(jnp.int32), jax.random.fold_in(splits[5], 1), 0, 1),
    }


def reference(integrals, block_list, p_slot, metric, density_panel, pattern):
    masked = jnp.where(pattern[:, None] > 0, density_panel, jnp.zeros_like(density_panel))
    panels = masked.reshape(NBLK, BS, OCC)
    slots_all = p_slot[block_list[:, 2]]
    per_group = N_COL * E_DEV
    factor = 1.0 / (NPB * BS * OCC)

    def one_group(group_index):
        first_row = group_index * per_group
        blocks_here = lax.dynamic_slice_in_dim(integrals, first_row, per_group, 0)
        lists_here = lax.dynamic_slice_in_dim(block_list, first_row, per_group, 0)
        slots_here = lax.dynamic_slice_in_dim(slots_all, first_row, per_group, 0)

        def accumulate(running, inputs_now):
            one_block, entry_ids, target = inputs_now
            offset = ((entry_ids[0] - group_index * MB) * BS).astype(jnp.int32)
            applied = jnp.einsum("qp,qx->px", metric[target].astype(jnp.float32), one_block.astype(jnp.float32)).astype(jnp.bfloat16)
            applied = lax.optimization_barrier(applied).astype(jnp.float32).reshape(BS, BS, BS)
            contrib = jnp.einsum("pmn,no->pmo", applied, panels[entry_ids[1]].astype(jnp.float32))
            anchor = jnp.zeros((), jnp.int32)
            corner = (target.astype(jnp.int32), anchor, offset, anchor)
            current = lax.dynamic_slice(running, corner, (1, BS, BS, OCC))
            return lax.dynamic_update_slice(running, current + contrib[None], corner), None

        empty_sum = jnp.zeros((NPB, BS, MB * BS, OCC), jnp.float32)
        filled, _ = lax.scan(accumulate, empty_sum, (blocks_here, lists_here, slots_here))
        rounded = lax.optimization_barrier(filled.astype(jnp.bfloat16)).astype(jnp.float32)
        return jnp.einsum("jpxo,jpzo->xz", rounded, rounded) * factor

    row_tiles = lax.map(one_group, jnp.arange(N_ROW, dtype=jnp.int32))
    return row_tiles.reshape(N_ROW * MB * BS, MB * BS)
```

```python
import functools

import jax
import jax.numpy as jnp
from jax import lax
from jax.experimental import pallas as pl
from jax.experimental.pallas import tpu as pltpu
from jax.sharding import PartitionSpec as P

MB = 8
LANES = 128
DEPTH = 2
PLACES = 16
BATCH = 4
MESH = pl.DeviceIdType.MESH
ANY = pl.BlockSpec(memory_space=pl.ANY)
VMEM = pl.BlockSpec(memory_space=pltpu.VMEM)
SMEM = pl.BlockSpec(memory_space=pltpu.SMEM)


def spread_kernel(axis, count, *refs):
    sources, targets = refs[:count], refs[count : 2 * count]
    sends, recvs, local = refs[2 * count :]
    me = lax.axis_index(axis)
    others = range(1, lax.axis_size(axis))

    def device(b):
        return {axis: lax.bitwise_xor(me, b)}

    barrier = pltpu.get_barrier_semaphore()
    for b in others:
        pl.semaphore_signal(barrier, inc=1, device_id=device(b), device_id_type=MESH)
    own = [
        pltpu.make_async_copy(source, target.at[me], local.at[k])
        for k, (source, target) in enumerate(zip(sources, targets))
    ]
    for copy in own:
        copy.start()
    pl.semaphore_wait(barrier, len(others))
    copies = []
    for k, (source, target) in enumerate(zip(sources, targets)):
        for b in others:
            copies.append(pltpu.make_async_remote_copy(
                source, target.at[me], sends.at[k, b], recvs.at[k, b],
                device_id=device(b), device_id_type=MESH))
            copies[-1].start()
    for copy in own + copies:
        copy.wait()


def spread(axis, size, number, arrays):
    count = len(arrays)
    return pl.pallas_call(
        functools.partial(spread_kernel, axis, count),
        out_shape=tuple(jax.ShapeDtypeStruct((size,) + a.shape, a.dtype) for a in arrays),
        in_specs=[VMEM] * count,
        out_specs=(VMEM,) * count,
        scratch_shapes=[
            pltpu.SemaphoreType.DMA((count, size)),
            pltpu.SemaphoreType.DMA((count, size)),
            pltpu.SemaphoreType.DMA((count,)),
        ],
        compiler_params=pltpu.CompilerParams(collective_id=number, has_side_effects=True),
        name="spread_" + axis,
    )(*arrays)


def apply_kernel(cols, depth, slot_ref, pick_ref, metric_ref, block_ref, *refs):
    outs, chosen, turned = refs[:cols], refs[cols], refs[cols + 1]
    lines = block_ref.shape[2] // LANES
    here = block_ref.shape[0]

    @pl.when(pl.program_id(0) == 0)
    def _():
        for e in range(chosen.shape[0]):
            chosen[e] = lax.dot_general(
                pick_ref[...], metric_ref[slot_ref[e]], (((1,), (1,)), ((), ())),
                preferred_element_type=jnp.float32).astype(jnp.bfloat16)

    for k in range(here):
        made = jnp.dot(
            chosen[pl.program_id(0) * here + k], block_ref[k], preferred_element_type=jnp.float32)
        total = made.shape[0]
        for start in range(0, total, 8):
            size = min(8, total - start)
            for line in range(lines):
                turned[k, pl.ds(start * lines + line, size, stride=lines), :] = made[
                    start : start + size, line * LANES : (line + 1) * LANES]
        for d in range(cols):
            for i in range(depth):
                row = (d * depth + i) * lines
                outs[d][i, k] = turned[k, row : row + lines, :].astype(jnp.bfloat16)


def apply_metric(cols, slot_ids, pick, metrics, integrals):
    listed, block_size, flat = integrals.shape
    lines = flat // LANES
    depth = pick.shape[0] // cols
    here = 3 if listed % 3 == 0 else 1
    shape = jax.ShapeDtypeStruct((depth, listed, lines, LANES), jnp.bfloat16)
    return pl.pallas_call(
        functools.partial(apply_kernel, cols, depth),
        grid=(listed // here,),
        out_shape=(shape,) * cols,
        in_specs=[SMEM, VMEM, VMEM, pl.BlockSpec((here, block_size, flat), lambda e: (e, 0, 0))],
        out_specs=(pl.BlockSpec((depth, here, lines, LANES), lambda e: (0, e, 0, 0)),) * cols,
        scratch_shapes=[
            pltpu.VMEM((listed, cols * depth, block_size), jnp.bfloat16),
            pltpu.VMEM((here, cols * depth * lines, LANES), jnp.float32),
        ],
        cost_estimate=pl.CostEstimate(flops=10**9, bytes_accessed=8 * 2**20, transcendentals=0),
        name="apply_metric",
    )(slot_ids, pick, metrics, integrals)


def build_kernel(cols, sizes, first, scale, corner_ref, second_ref, panel_ref, tile_ref, *refs):
    chunks, out_ref, acc = refs[:cols], refs[cols], refs[cols + 1]
    slots, side, block_size = sizes
    depth, listed, lines, _ = chunks[0].shape
    parity = LANES // block_size
    step = 6 if listed % 6 == 0 else 1
    acc[...] = jnp.zeros_like(acc)
    for d in range(cols):
        def entries(at, carry, d=d):
            made = []
            for k in range(step):
                e = at * step + k
                rows = chunks[d][:, pl.ds(e, 1)].reshape(depth * lines, LANES)
                made.append(jnp.dot(
                    rows, panel_ref[second_ref[d * listed + e]], preferred_element_type=jnp.float32))
            for k in range(step):
                corner = corner_ref[d * listed + at * step + k]
                for i in range(depth):
                    for odd in range(parity):
                        where = pl.ds(corner + odd, lines, stride=parity)
                        acc[i, where, :] += made[k][
                            i * lines : (i + 1) * lines, odd * LANES : (odd + 1) * LANES]
            return carry

        lax.fori_loop(0, listed // step, entries, 0)

    half = side // 2
    corners = ((0, 0), (0, 1), (1, 1))
    for a, b in corners:
        at = (slice(a * half, (a + 1) * half), slice(b * half, (b + 1) * half))
        out_ref[at] = jnp.zeros((half, half), jnp.float32) if first else tile_ref[at]
    batch = 4

    def products(group, carry):
        wide = jnp.concatenate(
            [
                acc[i, pl.ds(pl.multiple_of((group * batch + k) * side, side), side), :].astype(jnp.bfloat16)
                for k in range(batch)
                for i in range(depth)
            ],
            axis=1,
        )
        for a, b in corners:
            at = (slice(a * half, (a + 1) * half), slice(b * half, (b + 1) * half))
            out_ref[at] += lax.dot_general(
                wide[a * half : (a + 1) * half], wide[b * half : (b + 1) * half],
                (((1,), (1,)), ((), ())), preferred_element_type=jnp.float32)
        return carry

    lax.fori_loop(0, slots // batch, products, 0)
    if scale is not None:
        for a, b in corners:
            at = (slice(a * half, (a + 1) * half), slice(b * half, (b + 1) * half))
            out_ref[at] = out_ref[at] * scale
        out_ref[half:, :half] = out_ref[:half, half:].T


def build(cols, sizes, first, scale, corner, second, panels, tile, chunks):
    slots, side, _ = sizes
    depth = chunks[0].shape[0]
    return pl.pallas_call(
        functools.partial(build_kernel, cols, sizes, first, scale),
        out_shape=jax.ShapeDtypeStruct((side, side), jnp.float32),
        in_specs=[SMEM, SMEM, VMEM, VMEM] + [VMEM] * cols,
        out_specs=VMEM,
        scratch_shapes=[pltpu.VMEM((depth, slots * side, LANES), jnp.float32)],
        compiler_params=pltpu.CompilerParams(vmem_limit_bytes=56 * 2**20),
        cost_estimate=pl.CostEstimate(flops=10**10, bytes_accessed=8 * 2**20, transcendentals=0),
        name="build_tile",
    )(corner, second, panels, tile, *chunks)


def reduce_kernel(cols, tile_ref, out_ref, landed, crossing, crossed, sends, recvs):
    me_row, me_col = lax.axis_index("row"), lax.axis_index("col")
    share = out_ref.shape[0]
    half = cols // 2
    opposite = lax.bitwise_xor(me_col, half)

    def rows_of(col):
        return pl.ds(pl.multiple_of(col * share, share), share)

    barrier = pltpu.get_barrier_semaphore()
    for d in range(1, half + 1):
        pl.semaphore_signal(
            barrier, inc=1, device_id=(me_row, lax.bitwise_xor(me_col, d)), device_id_type=MESH)
    pl.semaphore_wait(barrier, half)
    near = []
    for side in (1, 0):
        for d in range(1, half):
            peer = lax.bitwise_xor(me_col, d)
            near.append(pltpu.make_async_remote_copy(
                tile_ref.at[rows_of(lax.bitwise_xor(peer, side * half))], landed.at[side, d - 1],
                sends.at[side, d - 1], recvs.at[side, d - 1], device_id=(me_row, peer), device_id_type=MESH))
            near[-1].start()
    total = tile_ref[rows_of(opposite), :]
    for d in range(1, half):
        near[d - 1].wait_recv()
        total = total + landed[1, d - 1]
    crossing[...] = total
    total = tile_ref[rows_of(me_col), :]
    out_ref[...] = total
    far = pltpu.make_async_remote_copy(
        crossing, crossed, sends.at[0, half - 1], recvs.at[0, half - 1],
        device_id=(me_row, opposite), device_id_type=MESH)
    far.start()
    for d in range(1, half):
        near[half - 2 + d].wait_recv()
        total = total + landed[0, d - 1]
    far.wait_recv()
    out_ref[...] = total + crossed[...]
    for copy in near:
        copy.wait_send()
    far.wait_send()


def reduce_tiles(cols, tile):
    side = tile.shape[0]
    half = cols // 2
    return pl.pallas_call(
        functools.partial(reduce_kernel, cols),
        out_shape=jax.ShapeDtypeStruct((side // cols, side), jnp.float32),
        in_specs=[VMEM],
        out_specs=VMEM,
        scratch_shapes=[
            pltpu.VMEM((2, half - 1, side // cols, side), jnp.float32),
            pltpu.VMEM((side // cols, side), jnp.float32),
            pltpu.VMEM((side // cols, side), jnp.float32),
            pltpu.SemaphoreType.DMA((2, half)),
            pltpu.SemaphoreType.DMA((2, half)),
        ],
        compiler_params=pltpu.CompilerParams(collective_id=1, has_side_effects=True),
        name="reduce_tiles",
    )(tile)


def in_phases(integrals, block_list, p_slot, metric, density_panel, pattern):
    rows, cols = lax.axis_size("row"), lax.axis_size("col")
    me_col = lax.axis_index("col")
    owned_slots, block_size = metric.shape[0], metric.shape[1]
    listed = integrals.shape[0]
    panel_width = density_panel.shape[1]
    slots = owned_slots * cols
    side = MB * block_size
    mine = block_size // cols
    depth = DEPTH if mine % DEPTH == 0 else 1
    phases = mine // depth
    metrics, panels_col, patterns_col, lists_col = spread(
        "col", cols, 0, (metric, density_panel, pattern.reshape(1, -1), block_list))
    metrics = metrics.reshape(slots, block_size, block_size)
    slot_match = block_list[:, 2][:, None] == jnp.arange(slots, dtype=jnp.int32)[None, :]
    slot_ids = jnp.sum(jnp.where(slot_match, p_slot[None, :], 0), axis=1)

    offsets = jnp.arange(cols, dtype=jnp.int32)
    peers = lax.bitwise_xor(offsets, me_col)
    places = jnp.arange(block_size, dtype=jnp.int32)
    sent = []
    for phase in range(phases):
        wanted = (peers[:, None] * mine + phase * depth + jnp.arange(depth, dtype=jnp.int32)).reshape(-1)
        pick = (wanted[:, None] == places[None, :]).astype(jnp.bfloat16)
        outgoing = apply_metric(cols, slot_ids, pick, metrics, integrals)
        arrived = [outgoing[0]]
        for d in range(1, cols):
            arrived.append(lax.ppermute(outgoing[d], "col", [(c, c ^ d) for c in range(cols)]))
        sent.append(arrived)
        if phase == 0:
            panels_col, patterns_col, lists_col, _ = lax.optimization_barrier(
                (panels_col, patterns_col, lists_col, outgoing[1]))

    panel_all, pattern_all = spread("row", rows, 2, (panels_col, patterns_col))
    panel_all = panel_all.reshape(-1, panel_width)
    panel_all = jnp.where(pattern_all.reshape(-1, 1) > 0, panel_all, jnp.zeros_like(panel_all))
    lists_in = jnp.sum(
        jnp.where((peers[:, None] == offsets[None, :])[:, :, None, None], lists_col[None], 0), axis=1)
    lists_in = lists_in.reshape(cols * listed, 3)
    match_in = lists_in[:, 2][:, None] == jnp.arange(slots, dtype=jnp.int32)[None, :]
    slots_in = jnp.sum(jnp.where(match_in, p_slot[None, :], 0), axis=1)
    corner = slots_in * side + (lists_in[:, 0] - lax.axis_index("row") * MB) * block_size
    second = lists_in[:, 1]
    parity = LANES // block_size
    blocks = panel_all.reshape(-1, block_size, panel_width)
    panels = jnp.concatenate(
        [
            jnp.pad(blocks, ((0, 0), (0, 0), (k * panel_width, (parity - 1 - k) * panel_width)))
            for k in range(parity)
        ],
        axis=1,
    )
    tile = jnp.zeros((8, LANES), jnp.float32)
    for phase in range(phases):
        last = phase == phases - 1
        scale = 1.0 / (slots * block_size * panel_width) if last else None
        tile = build(
            cols, (slots, side, block_size), phase == 0, scale, corner, second, panels, tile, sent[phase])
    return reduce_tiles(cols, tile)


def shapes_allow(rows, cols, listed, block_size, owned_slots, local_rows, panel_width, flat):
    slots = owned_slots * cols
    return (
        listed <= PLACES
        and listed % 2 == 0
        and cols * PLACES <= LANES
        and slots * MB <= LANES
        and slots % BATCH == 0
        and local_rows == block_size
        and rows * cols <= LANES
        and 2 * block_size == LANES
        and panel_width == LANES
        and flat == block_size * block_size
        and block_size % (cols * DEPTH) == 0
        and cols * DEPTH == 16
    )


def fused_kernel(rows, cols, cap, list_ref, slot_ref, pattern_ref, density_ref, metric_ref, integrals_ref,
                 out_ref, flag_ref, meta, metrics, panels, blocks, chosen, made, pick, turned, leaving,
                 arriving, places, table, entry, packed, terms, halves, tile, landed, crossing, crossed,
                 loads, near_send, near_recv, row_send, row_recv, sends, recvs, red_send, red_recv, moved):
    f32, bf16, i32 = jnp.float32, jnp.bfloat16, jnp.int32
    me_row, me_col = lax.axis_index("row"), lax.axis_index("col")
    me = me_row * cols + me_col
    listed, block_size, flat = blocks.shape
    slots = metrics.shape[0]
    owned = slots // cols
    lines = flat // LANES
    phases = block_size // (cols * DEPTH)
    devices = rows * cols
    tiles = cap // LANES
    side = MB * block_size
    others = tuple(range(cols // 2, cols)) + tuple(range(1, cols // 2))

    def col_peer(d):
        return (me_row, lax.bitwise_xor(me_col, d))

    def row_peer(d):
        return (lax.bitwise_xor(me_row, d), me_col)

    fetches = [pltpu.make_async_copy(integrals_ref.at[e], blocks.at[e], loads.at[e]) for e in range(listed)]
    for fetch in fetches:
        fetch.start()
    barrier = pltpu.get_barrier_semaphore()
    for d in range(1, cols):
        pl.semaphore_signal(barrier, inc=1, device_id=col_peer(d), device_id_type=MESH)
    for d in range(1, rows):
        pl.semaphore_signal(barrier, inc=1, device_id=row_peer(d), device_id_type=MESH)

    lane = lax.broadcasted_iota(i32, (1, LANES), 1)
    meta[me] = jnp.zeros(meta.shape[1:], i32)
    for e in range(PLACES):
        if e < listed:
            key = slot_ref[list_ref[e, 2]] * MB + list_ref[e, 0] - me_row * MB
            meta[me, e : e + 1, :] = jnp.where(lane < block_size, key, list_ref[e, 1])
        else:
            meta[me, e : e + 1, :] = jnp.where(lane < block_size, 4 * LANES, 0)
    pattern = (pattern_ref[...] > 0).astype(i32)
    meta[me, PLACES : PLACES + 1, :block_size] = pattern
    eye = lax.broadcasted_iota(i32, (block_size, block_size), 0) == lax.broadcasted_iota(
        i32, (block_size, block_size), 1)
    keep = jnp.sum(
        jnp.where(eye, jnp.broadcast_to(pattern.astype(f32), (block_size, block_size)), 0.0), axis=1, keepdims=True)
    panels[me] = jnp.where(keep > 0, density_ref[...].astype(f32), 0.0).astype(bf16)
    metrics[pl.ds(me_col * owned, owned)] = metric_ref[...]

    pl.semaphore_wait(barrier, cols - 1 + rows - 1)
    first = []
    for k, (source, target) in enumerate((
        (metric_ref, metrics.at[pl.ds(me_col * owned, owned)]),
        (meta.at[me], meta.at[me]),
        (panels.at[me], panels.at[me]),
    )):
        for d in others:
            first.append(pltpu.make_async_remote_copy(
                source, target, near_send.at[k, d], near_recv.at[k, d],
                device_id=col_peer(d), device_id_type=MESH))
            first[-1].start()
    for copy in first[: cols - 1]:
        copy.wait_recv()

    wanted = lax.broadcasted_iota(i32, (block_size, block_size), 0)
    wanted = (wanted // DEPTH % cols) * (block_size // cols) + wanted // (cols * DEPTH) * DEPTH + wanted % DEPTH
    order = (wanted == lax.broadcasted_iota(i32, (block_size, block_size), 1)).astype(bf16)
    for e in range(listed):
        chosen[e] = lax.dot_general(
            order, metrics[slot_ref[list_ref[e, 2]]], (((1,), (1,)), ((), ())),
            preferred_element_type=f32).astype(bf16)

    def apply(e, carry):
        pltpu.make_async_copy(integrals_ref.at[e], blocks.at[e], loads.at[e]).wait()
        for j in range(lines // 2):
            value = jnp.dot(
                chosen[e], blocks[e, :, 2 * j * LANES : 2 * (j + 1) * LANES],
                preferred_element_type=f32).astype(bf16)
            for p in range(phases):
                for h in range(2):
                    made[p, e, (2 * j + h) * 16 : (2 * j + h + 1) * 16, :] = value[
                        p * 16 : (p + 1) * 16, h * LANES : (h + 1) * LANES]
        return carry

    split = listed // 3
    lax.fori_loop(0, split, apply, 0)
    for copy in first[cols - 1 :]:
        copy.wait_recv()
    second = []
    group = pl.ds(me_row * cols, cols)
    for k, ref in enumerate((meta, panels)):
        for d in range(rows - 1, 0, -1):
            second.append(pltpu.make_async_remote_copy(
                ref.at[group], ref.at[group], row_send.at[k, d], row_recv.at[k, d],
                device_id=row_peer(d), device_id_type=MESH))
            second[-1].start()
    lax.fori_loop(split, listed, apply, 0)
    for copy in second[: rows - 1]:
        copy.wait_recv()

    square = (LANES, LANES)
    down, across = lax.broadcasted_iota(i32, square, 0), lax.broadcasted_iota(i32, square, 1)
    kept = jnp.concatenate(
        [
            jnp.where(
                lax.broadcasted_iota(i32, (devices, LANES), 1) < block_size, meta[:, PLACES, :], 0).astype(f32),
            jnp.zeros((LANES - devices, LANES), f32),
        ],
        axis=0,
    ) if devices < LANES else jnp.where(across < block_size, meta[:, PLACES, :], 0).astype(f32)
    running = jnp.dot(kept.astype(bf16), (down <= across).astype(bf16), preferred_element_type=f32)
    ranks = jnp.where(kept > 0, running - 1.0, -256.0).astype(bf16)
    mine = meta[group, :PLACES, :].reshape(cols * PLACES, LANES)
    mine = mine if cols * PLACES == LANES else jnp.concatenate(
        [mine, jnp.full((LANES - cols * PLACES, LANES), 4 * LANES, i32)], axis=0)
    key = mine[:, 0:1]
    panel_of = mine[:, block_size : block_size + 1]
    real = (down[:, 0:1] % PLACES < listed) & (down[:, 0:1] < cols * PLACES)
    hot = ((panel_of == across) & real).astype(bf16)
    counts = jnp.sum(jnp.dot(hot, kept.astype(bf16), preferred_element_type=f32), axis=1, keepdims=True)
    ahead = ((down // PLACES == across // PLACES) & (across < down)).astype(bf16)
    starts = jnp.dot(ahead, jnp.broadcast_to(counts, square).astype(bf16), preferred_element_type=f32)
    rank = jnp.dot(hot, ranks, preferred_element_type=f32)
    places[...] = jnp.where(real & (rank >= 0) & (across < block_size), rank + starts, -1.0)

    def choose(e, carry):
        spot = jnp.broadcast_to(places[pl.ds(me_col * PLACES + e, 1), :], (block_size, LANES))
        half = lax.broadcasted_iota(i32, (block_size, LANES), 1)
        spot = jnp.sum(
            jnp.where(lax.broadcasted_iota(i32, (block_size, LANES), 0) == half, spot, 0.0), axis=1, keepdims=True)
        for t in range(tiles):
            block = (spot == (half + t * LANES).astype(f32)).astype(f32).astype(bf16)
            for odd in range(2):
                pick[odd * tiles + t, e, odd * block_size : (odd + 1) * block_size, :] = block
                pick[odd * tiles + t, e, (1 - odd) * block_size : (2 - odd) * block_size, :] = jnp.zeros_like(block)
        return carry

    lax.fori_loop(0, listed, choose, 0)

    def pack(p, carry):
        def columns(nb, inner):
            right = jnp.concatenate(
                [
                    pick[2 * nb].reshape(listed * LANES, LANES),
                    pick[2 * nb + 1].reshape(listed * LANES, LANES),
                ],
                axis=1,
            )
            for part in range(lines * 16 // 256):
                left = jnp.concatenate(
                    [made[p, e, part * 256 : (part + 1) * 256, :] for e in range(listed)], axis=1)
                value = jnp.dot(left, right, preferred_element_type=f32)
                for line in range(16):
                    for g in range(2):
                        for h in range(2):
                            turned[2 * nb + h, pl.ds(g * 8 * lines + part * 16 + line, 8, stride=lines), :] = value[
                                line * 16 + g * 8 : line * 16 + g * 8 + 8, h * LANES : (h + 1) * LANES]
            return inner

        lax.fori_loop(0, tiles, columns, 0)
        for c in range(cols):
            for i in range(DEPTH):
                row = (c * DEPTH + i) * lines
                leaving[p, c, i] = turned[:, row : row + lines, :].astype(bf16)
        for d in others:
            pltpu.make_async_remote_copy(
                leaving.at[p, lax.bitwise_xor(me_col, d)], arriving.at[p, me_col], sends.at[p, d], recvs.at[p, d],
                device_id=col_peer(d), device_id_type=MESH).start()
        arriving[p, me_col] = leaving[p, me_col]
        return carry

    lax.fori_loop(0, phases, pack, 0)

    key_down = jnp.broadcast_to(key, square)
    key_across = jnp.broadcast_to(
        jnp.sum(jnp.where(down == across, key_down, 0), axis=0, keepdims=True), square)
    same_before = jnp.where((key_down == key_across) & (across < down), 1, 0)
    before = jnp.where(key_across < key_down, 1, 0) + same_before
    position = jnp.sum(before, axis=1, keepdims=True)
    repeats = jnp.minimum(jnp.sum(same_before, axis=1, keepdims=True), 1)
    at = position == across
    compact = down // PLACES * listed + down % PLACES
    table[0:1, :] = jnp.sum(jnp.where(at, compact, 0), axis=0, keepdims=True)
    table[1:2, :] = jnp.sum(jnp.where(at, repeats, 0), axis=0, keepdims=True)
    upto = jnp.sum(jnp.where(key_down <= across, 1, 0), axis=0, keepdims=True) - 1
    present = jnp.sum(jnp.where(key_down == across, 1, 0), axis=0, keepdims=True)
    table[2:3, :] = jnp.where(present > 0, upto, cols * listed)
    table[3:4, :] = jnp.sum(jnp.where(down == across, panel_of, 0), axis=0, keepdims=True)
    table[4:8, :] = jnp.zeros((4, LANES), i32)
    down_table = pltpu.make_async_copy(table, entry, moved)
    down_table.start()

    entries = meta[:, :PLACES, :].reshape(devices * PLACES, LANES)
    wide = (devices * PLACES, LANES)
    row_id = lax.broadcasted_iota(i32, wide, 0)
    hot_all = (
        (entries[:, block_size : block_size + 1] == lax.broadcasted_iota(i32, wide, 1)) & (row_id % PLACES < listed)
    ).astype(bf16)
    sizes = jnp.dot(hot_all, kept.astype(bf16), preferred_element_type=f32)
    owner = lax.broadcasted_iota(i32, (devices, devices * PLACES), 1) // PLACES
    owner = (owner == lax.broadcasted_iota(i32, (devices, devices * PLACES), 0)).astype(bf16)
    totals = jnp.sum(jnp.dot(owner, sizes.astype(bf16), preferred_element_type=f32), axis=1, keepdims=True)
    worst = jnp.max(jnp.broadcast_to(totals, (devices, LANES)), axis=0, keepdims=True)
    flag_ref[...] = jnp.broadcast_to((worst <= cap).astype(i32), flag_ref.shape)

    halves[cols * listed] = jnp.zeros((DEPTH, block_size, LANES), bf16)
    for a in range(2):
        tile[a * (side // 2) : (a + 1) * (side // 2), :] = jnp.zeros((side // 2, side), f32)
    down_table.wait()
    for copy in second[rows - 1 :]:
        copy.wait_recv()

    def gather(at_pair, carry):
        c, pair = at_pair // (listed // 2), at_pair % (listed // 2)
        for h in range(2):
            place = c * PLACES + pair * 2 + h
            spot = jnp.broadcast_to(places[pl.ds(place, 1), :][:, :block_size], (cap, block_size))
            chosen_rows = (spot == lax.broadcasted_iota(i32, (cap, block_size), 0).astype(f32)).astype(f32).astype(bf16)
            packed[c, pair, :, h * LANES : (h + 1) * LANES] = jnp.dot(
                chosen_rows, panels[entry[3, place]], preferred_element_type=f32).astype(bf16)
        return carry

    lax.fori_loop(0, cols * (listed // 2), gather, 0)

    def phase(p, carry):
        def source(d, inner):
            c = lax.bitwise_xor(me_col, d)

            @pl.when(d > 0)
            def _():
                pltpu.make_async_remote_copy(
                    leaving.at[p, c], arriving.at[p, c], sends.at[p, d], recvs.at[p, d],
                    device_id=(me_row, c), device_id_type=MESH).wait_recv()

            left = jnp.concatenate(
                [
                    jnp.concatenate([arriving[p, c, i, odd * tiles + t] for t in range(tiles)], axis=1)
                    for odd in range(2)
                    for i in range(DEPTH)
                ],
                axis=0,
            )
            for pair in range(listed // 2):
                value = jnp.dot(left, packed[c, pair], preferred_element_type=f32)
                for h in range(2):
                    for odd in range(2):
                        for i in range(DEPTH):
                            row = (odd * DEPTH + i) * lines
                            terms[c * listed + pair * 2 + h, i, pl.ds(odd, lines, stride=2), :] = value[row : row + lines, h * LANES : (h + 1) * LANES]
            return inner

        lax.fori_loop(0, cols, source, 0)

        def segment(r, total):
            for k in range(4):
                at = r * 4 + k
                again = entry[1, at].astype(f32)
                total = terms[entry[0, at]] + total * again
                halves[at] = total.astype(bf16)
            return total

        lax.fori_loop(0, cols * listed // 4, segment, jnp.zeros((DEPTH, block_size, LANES), f32))

        def products(s, inner):
            strip = []
            for a in range(MB):
                parts = []
                for k in range(BATCH):
                    cell = halves[entry[2, (s * BATCH + k) * MB + a]]
                    parts.extend(cell[i] for i in range(DEPTH))
                strip.append(jnp.concatenate(parts, axis=1))
            high = jnp.concatenate(strip[: MB // 2], axis=0)
            low = jnp.concatenate(strip[MB // 2 :], axis=0)
            half = side // 2
            for left, right, a, b in ((high, high, 0, 0), (high, low, 0, 1), (low, low, 1, 1)):
                tile[a * half : (a + 1) * half, b * half : (b + 1) * half] += lax.dot_general(
                    left, right, (((1,), (1,)), ((), ())), preferred_element_type=f32)
            return inner

        lax.fori_loop(0, slots // BATCH, products, 0)
        return carry

    lax.fori_loop(0, phases, phase, 0)
    half = side // 2
    tile[half:, :half] = tile[:half, half:].T

    scale = 1.0 / (slots * block_size * LANES)
    share = out_ref.shape[0]
    middle = cols // 2
    opposite = lax.bitwise_xor(me_col, middle)

    def rows_of(col):
        return pl.ds(pl.multiple_of(col * share, share), share)

    near = []
    for far_side in (1, 0):
        for d in range(1, middle):
            peer = lax.bitwise_xor(me_col, d)
            near.append(pltpu.make_async_remote_copy(
                tile.at[rows_of(lax.bitwise_xor(peer, far_side * middle))], landed.at[far_side, d - 1],
                red_send.at[far_side, d - 1], red_recv.at[far_side, d - 1],
                device_id=(me_row, peer), device_id_type=MESH))
            near[-1].start()
    total = tile[rows_of(opposite), :]
    for d in range(1, middle):
        near[d - 1].wait_recv()
        total = total + landed[1, d - 1]
    crossing[...] = total
    far = pltpu.make_async_remote_copy(
        crossing, crossed, red_send.at[0, middle - 1], red_recv.at[0, middle - 1],
        device_id=(me_row, opposite), device_id_type=MESH)
    far.start()
    total = tile[rows_of(me_col), :]
    for d in range(1, middle):
        near[middle - 2 + d].wait_recv()
        total = total + landed[0, d - 1]
    far.wait_recv()
    out_ref[...] = (total + crossed[...]) * scale
    for copy in first + second + near + [far]:
        copy.wait_send()

    def finish(p, carry):
        for d in others:
            c = lax.bitwise_xor(me_col, d)
            pltpu.make_async_remote_copy(
                leaving.at[p, c], arriving.at[p, me_col], sends.at[p, d], recvs.at[p, d],
                device_id=(me_row, c), device_id_type=MESH).wait_send()
        return carry

    lax.fori_loop(0, phases, finish, 0)


def fused(integrals, block_list, p_slot, metric, density_panel, pattern):
    rows, cols = lax.axis_size("row"), lax.axis_size("col")
    listed, block_size, flat = integrals.shape
    slots = metric.shape[0] * cols
    devices = rows * cols
    side = MB * block_size
    lines = flat // LANES
    phases = block_size // (cols * DEPTH)
    cap = -(-(listed * block_size * 5 // 6) // LANES) * LANES
    tiles = cap // LANES
    bf16, f32, i32 = jnp.bfloat16, jnp.float32, jnp.int32
    half = cols // 2
    dma = pltpu.SemaphoreType.DMA
    out, flag = pl.pallas_call(
        functools.partial(fused_kernel, rows, cols, cap),
        out_shape=(
            jax.ShapeDtypeStruct((side // cols, side), f32),
            jax.ShapeDtypeStruct((8, LANES), i32),
        ),
        in_specs=[SMEM, SMEM, VMEM, VMEM, VMEM, ANY],
        out_specs=(VMEM, VMEM),
        scratch_shapes=[
            pltpu.VMEM((devices, PLACES + 8, LANES), i32),
            pltpu.VMEM((slots, block_size, block_size), bf16),
            pltpu.VMEM((devices, block_size, LANES), bf16),
            pltpu.VMEM((listed, block_size, flat), bf16),
            pltpu.VMEM((listed, block_size, block_size), bf16),
            pltpu.VMEM((phases, listed, lines * 16, LANES), bf16),
            pltpu.VMEM((2 * tiles, listed, LANES, LANES), bf16),
            pltpu.VMEM((2 * tiles, 16 * lines, LANES), f32),
            pltpu.VMEM((phases, cols, DEPTH, 2 * tiles, lines, LANES), bf16),
            pltpu.VMEM((phases, cols, DEPTH, 2 * tiles, lines, LANES), bf16),
            pltpu.VMEM((LANES, LANES), f32),
            pltpu.VMEM((8, LANES), i32),
            pltpu.SMEM((8, LANES), i32),
            pltpu.VMEM((cols, listed // 2, cap, 2 * LANES), bf16),
            pltpu.VMEM((cols * listed, DEPTH, block_size, LANES), f32),
            pltpu.VMEM((cols * listed + 1, DEPTH, block_size, LANES), bf16),
            pltpu.VMEM((side, side), f32),
            pltpu.VMEM((2, half - 1, side // cols, side), f32),
            pltpu.VMEM((side // cols, side), f32),
            pltpu.VMEM((side // cols, side), f32),
            dma((listed,)),
            dma((3, cols)),
            dma((3, cols)),
            dma((2, rows)),
            dma((2, rows)),
            dma((phases, cols)),
            dma((phases, cols)),
            dma((2, half)),
            dma((2, half)),
            dma,
        ],
        compiler_params=pltpu.CompilerParams(
            collective_id=3, has_side_effects=True, vmem_limit_bytes=63 * 2**20),
        name="fused",
    )(block_list, p_slot, pattern.reshape(1, -1), density_panel, metric, integrals)
    return out, flag


def on_device(integrals, block_list, p_slot, metric, density_panel, pattern):
    arguments = (integrals, block_list, p_slot, metric, density_panel, pattern)
    listed, block_size, flat = integrals.shape
    if not shapes_allow(
        lax.axis_size("row"), lax.axis_size("col"), listed, block_size, metric.shape[0],
        density_panel.shape[0], density_panel.shape[1], flat,
    ):
        return in_phases(*arguments)
    out, flag = fused(*arguments)
    return lax.cond(flag[0, 0] > 0, lambda *_: out, in_phases, *arguments)


def solution(mesh):
    placed = (
        P(("row", "col"), None, None),
        P(("row", "col"), None),
        P(),
        P("col", None, None),
        P(("row", "col"), None),
        P(("row", "col")),
    )
    return jax.shard_map(
        on_device, mesh=mesh, in_specs=placed, out_specs=P(("row", "col"), None), check_vma=False
    )
```

```python
import functools

import jax
import jax.numpy as jnp
from jax import lax
from jax.experimental import pallas as pl
from jax.experimental.pallas import tpu as pltpu
from jax.sharding import PartitionSpec as P

MB = 8
LANES = 128
DEPTH = 2
PLACES = 16
BATCH = 4
MESH = pl.DeviceIdType.MESH
ANY = pl.BlockSpec(memory_space=pl.ANY)
VMEM = pl.BlockSpec(memory_space=pltpu.VMEM)
SMEM = pl.BlockSpec(memory_space=pltpu.SMEM)


def spread_kernel(axis, count, *refs):
    sources, targets = refs[:count], refs[count : 2 * count]
    sends, recvs, local = refs[2 * count :]
    me = lax.axis_index(axis)
    others = range(1, lax.axis_size(axis))

    def device(b):
        return {axis: lax.bitwise_xor(me, b)}

    barrier = pltpu.get_barrier_semaphore()
    for b in others:
        pl.semaphore_signal(barrier, inc=1, device_id=device(b), device_id_type=MESH)
    own = [
        pltpu.make_async_copy(source, target.at[me], local.at[k])
        for k, (source, target) in enumerate(zip(sources, targets))
    ]
    for copy in own:
        copy.start()
    pl.semaphore_wait(barrier, len(others))
    copies = []
    for k, (source, target) in enumerate(zip(sources, targets)):
        for b in others:
            copies.append(pltpu.make_async_remote_copy(
                source, target.at[me], sends.at[k, b], recvs.at[k, b],
                device_id=device(b), device_id_type=MESH))
            copies[-1].start()
    for copy in own + copies:
        copy.wait()


def spread(axis, size, number, arrays):
    count = len(arrays)
    return pl.pallas_call(
        functools.partial(spread_kernel, axis, count),
        out_shape=tuple(jax.ShapeDtypeStruct((size,) + a.shape, a.dtype) for a in arrays),
        in_specs=[VMEM] * count,
        out_specs=(VMEM,) * count,
        scratch_shapes=[
            pltpu.SemaphoreType.DMA((count, size)),
            pltpu.SemaphoreType.DMA((count, size)),
            pltpu.SemaphoreType.DMA((count,)),
        ],
        compiler_params=pltpu.CompilerParams(collective_id=number, has_side_effects=True),
        name="spread_" + axis,
    )(*arrays)


def apply_kernel(cols, depth, slot_ref, pick_ref, metric_ref, block_ref, *refs):
    outs, chosen, turned = refs[:cols], refs[cols], refs[cols + 1]
    lines = block_ref.shape[2] // LANES
    here = block_ref.shape[0]

    @pl.when(pl.program_id(0) == 0)
    def _():
        for e in range(chosen.shape[0]):
            chosen[e] = lax.dot_general(
                pick_ref[...], metric_ref[slot_ref[e]], (((1,), (1,)), ((), ())),
                preferred_element_type=jnp.float32).astype(jnp.bfloat16)

    for k in range(here):
        made = jnp.dot(
            chosen[pl.program_id(0) * here + k], block_ref[k], preferred_element_type=jnp.float32)
        total = made.shape[0]
        for start in range(0, total, 8):
            size = min(8, total - start)
            for line in range(lines):
                turned[k, pl.ds(start * lines + line, size, stride=lines), :] = made[
                    start : start + size, line * LANES : (line + 1) * LANES]
        for d in range(cols):
            for i in range(depth):
                row = (d * depth + i) * lines
                outs[d][i, k] = turned[k, row : row + lines, :].astype(jnp.bfloat16)


def apply_metric(cols, slot_ids, pick, metrics, integrals):
    listed, block_size, flat = integrals.shape
    lines = flat // LANES
    depth = pick.shape[0] // cols
    here = 3 if listed % 3 == 0 else 1
    shape = jax.ShapeDtypeStruct((depth, listed, lines, LANES), jnp.bfloat16)
    return pl.pallas_call(
        functools.partial(apply_kernel, cols, depth),
        grid=(listed // here,),
        out_shape=(shape,) * cols,
        in_specs=[SMEM, VMEM, VMEM, pl.BlockSpec((here, block_size, flat), lambda e: (e, 0, 0))],
        out_specs=(pl.BlockSpec((depth, here, lines, LANES), lambda e: (0, e, 0, 0)),) * cols,
        scratch_shapes=[
            pltpu.VMEM((listed, cols * depth, block_size), jnp.bfloat16),
            pltpu.VMEM((here, cols * depth * lines, LANES), jnp.float32),
        ],
        cost_estimate=pl.CostEstimate(flops=10**9, bytes_accessed=8 * 2**20, transcendentals=0),
        name="apply_metric",
    )(slot_ids, pick, metrics, integrals)


def build_kernel(cols, sizes, first, scale, corner_ref, second_ref, panel_ref, tile_ref, *refs):
    chunks, out_ref, acc = refs[:cols], refs[cols], refs[cols + 1]
    slots, side, block_size = sizes
    depth, listed, lines, _ = chunks[0].shape
    parity = LANES // block_size
    step = 6 if listed % 6 == 0 else 1
    acc[...] = jnp.zeros_like(acc)
    for d in range(cols):
        def entries(at, carry, d=d):
            made = []
            for k in range(step):
                e = at * step + k
                rows = chunks[d][:, pl.ds(e, 1)].reshape(depth * lines, LANES)
                made.append(jnp.dot(
                    rows, panel_ref[second_ref[d * listed + e]], preferred_element_type=jnp.float32))
            for k in range(step):
                corner = corner_ref[d * listed + at * step + k]
                for i in range(depth):
                    for odd in range(parity):
                        where = pl.ds(corner + odd, lines, stride=parity)
                        acc[i, where, :] += made[k][
                            i * lines : (i + 1) * lines, odd * LANES : (odd + 1) * LANES]
            return carry

        lax.fori_loop(0, listed // step, entries, 0)

    half = side // 2
    corners = ((0, 0), (0, 1), (1, 1))
    for a, b in corners:
        at = (slice(a * half, (a + 1) * half), slice(b * half, (b + 1) * half))
        out_ref[at] = jnp.zeros((half, half), jnp.float32) if first else tile_ref[at]
    batch = 4

    def products(group, carry):
        wide = jnp.concatenate(
            [
                acc[i, pl.ds(pl.multiple_of((group * batch + k) * side, side), side), :].astype(jnp.bfloat16)
                for k in range(batch)
                for i in range(depth)
            ],
            axis=1,
        )
        for a, b in corners:
            at = (slice(a * half, (a + 1) * half), slice(b * half, (b + 1) * half))
            out_ref[at] += lax.dot_general(
                wide[a * half : (a + 1) * half], wide[b * half : (b + 1) * half],
                (((1,), (1,)), ((), ())), preferred_element_type=jnp.float32)
        return carry

    lax.fori_loop(0, slots // batch, products, 0)
    if scale is not None:
        for a, b in corners:
            at = (slice(a * half, (a + 1) * half), slice(b * half, (b + 1) * half))
            out_ref[at] = out_ref[at] * scale
        out_ref[half:, :half] = out_ref[:half, half:].T


def build(cols, sizes, first, scale, corner, second, panels, tile, chunks):
    slots, side, _ = sizes
    depth = chunks[0].shape[0]
    return pl.pallas_call(
        functools.partial(build_kernel, cols, sizes, first, scale),
        out_shape=jax.ShapeDtypeStruct((side, side), jnp.float32),
        in_specs=[SMEM, SMEM, VMEM, VMEM] + [VMEM] * cols,
        out_specs=VMEM,
        scratch_shapes=[pltpu.VMEM((depth, slots * side, LANES), jnp.float32)],
        compiler_params=pltpu.CompilerParams(vmem_limit_bytes=56 * 2**20),
        cost_estimate=pl.CostEstimate(flops=10**10, bytes_accessed=8 * 2**20, transcendentals=0),
        name="build_tile",
    )(corner, second, panels, tile, *chunks)


def reduce_kernel(cols, tile_ref, out_ref, landed, crossing, crossed, sends, recvs):
    me_row, me_col = lax.axis_index("row"), lax.axis_index("col")
    share = out_ref.shape[0]
    half = cols // 2
    opposite = lax.bitwise_xor(me_col, half)

    def rows_of(col):
        return pl.ds(pl.multiple_of(col * share, share), share)

    barrier = pltpu.get_barrier_semaphore()
    for d in range(1, half + 1):
        pl.semaphore_signal(
            barrier, inc=1, device_id=(me_row, lax.bitwise_xor(me_col, d)), device_id_type=MESH)
    pl.semaphore_wait(barrier, half)
    near = []
    for side in (1, 0):
        for d in range(1, half):
            peer = lax.bitwise_xor(me_col, d)
            near.append(pltpu.make_async_remote_copy(
                tile_ref.at[rows_of(lax.bitwise_xor(peer, side * half))], landed.at[side, d - 1],
                sends.at[side, d - 1], recvs.at[side, d - 1], device_id=(me_row, peer), device_id_type=MESH))
            near[-1].start()
    total = tile_ref[rows_of(opposite), :]
    for d in range(1, half):
        near[d - 1].wait_recv()
        total = total + landed[1, d - 1]
    crossing[...] = total
    total = tile_ref[rows_of(me_col), :]
    out_ref[...] = total
    far = pltpu.make_async_remote_copy(
        crossing, crossed, sends.at[0, half - 1], recvs.at[0, half - 1],
        device_id=(me_row, opposite), device_id_type=MESH)
    far.start()
    for d in range(1, half):
        near[half - 2 + d].wait_recv()
        total = total + landed[0, d - 1]
    far.wait_recv()
    out_ref[...] = total + crossed[...]
    for copy in near:
        copy.wait_send()
    far.wait_send()


def reduce_tiles(cols, tile):
    side = tile.shape[0]
    half = cols // 2
    return pl.pallas_call(
        functools.partial(reduce_kernel, cols),
        out_shape=jax.ShapeDtypeStruct((side // cols, side), jnp.float32),
        in_specs=[VMEM],
        out_specs=VMEM,
        scratch_shapes=[
            pltpu.VMEM((2, half - 1, side // cols, side), jnp.float32),
            pltpu.VMEM((side // cols, side), jnp.float32),
            pltpu.VMEM((side // cols, side), jnp.float32),
            pltpu.SemaphoreType.DMA((2, half)),
            pltpu.SemaphoreType.DMA((2, half)),
        ],
        compiler_params=pltpu.CompilerParams(collective_id=1, has_side_effects=True),
        name="reduce_tiles",
    )(tile)


def in_phases(integrals, block_list, p_slot, metric, density_panel, pattern):
    rows, cols = lax.axis_size("row"), lax.axis_size("col")
    me_col = lax.axis_index("col")
    owned_slots, block_size = metric.shape[0], metric.shape[1]
    listed = integrals.shape[0]
    panel_width = density_panel.shape[1]
    slots = owned_slots * cols
    side = MB * block_size
    mine = block_size // cols
    depth = DEPTH if mine % DEPTH == 0 else 1
    phases = mine // depth
    metrics, panels_col, patterns_col, lists_col = spread(
        "col", cols, 0, (metric, density_panel, pattern.reshape(1, -1), block_list))
    metrics = metrics.reshape(slots, block_size, block_size)
    slot_match = block_list[:, 2][:, None] == jnp.arange(slots, dtype=jnp.int32)[None, :]
    slot_ids = jnp.sum(jnp.where(slot_match, p_slot[None, :], 0), axis=1)

    offsets = jnp.arange(cols, dtype=jnp.int32)
    peers = lax.bitwise_xor(offsets, me_col)
    places = jnp.arange(block_size, dtype=jnp.int32)
    sent = []
    for phase in range(phases):
        wanted = (peers[:, None] * mine + phase * depth + jnp.arange(depth, dtype=jnp.int32)).reshape(-1)
        pick = (wanted[:, None] == places[None, :]).astype(jnp.bfloat16)
        outgoing = apply_metric(cols, slot_ids, pick, metrics, integrals)
        arrived = [outgoing[0]]
        for d in range(1, cols):
            arrived.append(lax.ppermute(outgoing[d], "col", [(c, c ^ d) for c in range(cols)]))
        sent.append(arrived)
        if phase == 0:
            panels_col, patterns_col, lists_col, _ = lax.optimization_barrier(
                (panels_col, patterns_col, lists_col, outgoing[1]))

    panel_all, pattern_all = spread("row", rows, 2, (panels_col, patterns_col))
    panel_all = panel_all.reshape(-1, panel_width)
    panel_all = jnp.where(pattern_all.reshape(-1, 1) > 0, panel_all, jnp.zeros_like(panel_all))
    lists_in = jnp.sum(
        jnp.where((peers[:, None] == offsets[None, :])[:, :, None, None], lists_col[None], 0), axis=1)
    lists_in = lists_in.reshape(cols * listed, 3)
    match_in = lists_in[:, 2][:, None] == jnp.arange(slots, dtype=jnp.int32)[None, :]
    slots_in = jnp.sum(jnp.where(match_in, p_slot[None, :], 0), axis=1)
    corner = slots_in * side + (lists_in[:, 0] - lax.axis_index("row") * MB) * block_size
    second = lists_in[:, 1]
    parity = LANES // block_size
    blocks = panel_all.reshape(-1, block_size, panel_width)
    panels = jnp.concatenate(
        [
            jnp.pad(blocks, ((0, 0), (0, 0), (k * panel_width, (parity - 1 - k) * panel_width)))
            for k in range(parity)
        ],
        axis=1,
    )
    tile = jnp.zeros((8, LANES), jnp.float32)
    for phase in range(phases):
        last = phase == phases - 1
        scale = 1.0 / (slots * block_size * panel_width) if last else None
        tile = build(
            cols, (slots, side, block_size), phase == 0, scale, corner, second, panels, tile, sent[phase])
    return reduce_tiles(cols, tile)


def shapes_allow(rows, cols, listed, block_size, owned_slots, local_rows, panel_width, flat):
    slots = owned_slots * cols
    return (
        listed <= PLACES
        and listed % 4 == 0
        and cols * PLACES <= LANES
        and slots * MB <= LANES
        and slots % BATCH == 0
        and local_rows == block_size
        and rows * cols <= LANES
        and 2 * block_size == LANES
        and panel_width == LANES
        and flat == block_size * block_size
        and block_size % (cols * DEPTH) == 0
        and cols * DEPTH == 16
    )


def fused_kernel(rows, cols, cap, list_in, slot_in, pattern_in, density_in, metric_in, integrals_ref,
                 out_ref, flag_ref, list_ref, slot_ref, pattern_ref, density_ref, inputs, kept_rows, totals, lists, metrics, panels, blocks, chosen, made, pick, turned,
                 leaving, arriving, places, table, entry, packed, terms, halves, tile, landed, crossing, crossed,
                 loads, near_send, near_recv, row_send, row_recv, all_send, all_recv, sends, recvs, red_send,
                 red_recv, moved):
    f32, bf16, i32 = jnp.float32, jnp.bfloat16, jnp.int32
    me_row, me_col = lax.axis_index("row"), lax.axis_index("col")
    me = me_row * cols + me_col
    listed, block_size, flat = blocks.shape
    slots = metrics.shape[0]
    owned = slots // cols
    lines = flat // LANES
    phases = block_size // (cols * DEPTH)
    devices = rows * cols
    tiles = cap // LANES
    side = MB * block_size
    others = tuple(range(cols // 2, cols)) + tuple(range(1, cols // 2))
    everyone = [(r, c) for c in others + (0,) for r in range(rows) if r or c]

    def peer(r, c):
        return (lax.bitwise_xor(me_row, r), lax.bitwise_xor(me_col, c))

    barrier = pltpu.get_barrier_semaphore()
    for r, c in everyone:
        pl.semaphore_signal(barrier, inc=1, device_id=peer(r, c), device_id_type=MESH)
    own = pl.ds(me_col * owned, owned)
    small = [
        pltpu.make_async_copy(source, target, inputs.at[k])
        for k, (source, target) in enumerate((
            (pattern_in, pattern_ref),
            (list_in, list_ref),
            (slot_in, slot_ref),
            (metric_in, metrics.at[own]),
            (density_in, density_ref),
        ))
    ]
    fetches = [pltpu.make_async_copy(integrals_ref.at[e], blocks.at[e], loads.at[e]) for e in range(listed)]
    for fetch in small + fetches:
        fetch.start()
    for fetch in small:
        fetch.wait()

    lane = lax.broadcasted_iota(i32, (1, LANES), 1)
    for e in range(PLACES):
        if e < listed:
            key = slot_ref[list_ref[2, e]] * MB + list_ref[0, e] - me_row * MB
            lists[me_col, e : e + 1, :] = jnp.where(lane < block_size, key, list_ref[1, e])
        else:
            lists[me_col, e : e + 1, :] = jnp.where(lane < block_size, 4 * LANES, 0)
    pattern = (pattern_ref[...] > 0).astype(i32)
    kept_rows[me] = jnp.concatenate([pattern, jnp.zeros_like(pattern)], axis=1)
    eye = lax.broadcasted_iota(i32, (block_size, block_size), 0) == lax.broadcasted_iota(
        i32, (block_size, block_size), 1)
    keep = jnp.sum(
        jnp.where(eye, jnp.broadcast_to(pattern.astype(f32), (block_size, block_size)), 0.0), axis=1, keepdims=True)
    panels[me] = jnp.where(keep > 0, density_ref[...].astype(f32), 0.0).astype(bf16)
    wanted = lax.broadcasted_iota(i32, (block_size, block_size), 0)
    wanted = (wanted // DEPTH % cols) * (block_size // cols) + wanted // (cols * DEPTH) * DEPTH + wanted % DEPTH
    order = (wanted == lax.broadcasted_iota(i32, (block_size, block_size), 1)).astype(bf16)

    pl.semaphore_wait(barrier, devices - 1)

    def share(ref, target, k, peers, send_sems, recv_sems):
        copies = [
            pltpu.make_async_remote_copy(
                ref, target, send_sems.at[k, r * cols + c], recv_sems.at[k, r * cols + c],
                device_id=peer(r, c), device_id_type=MESH)
            for r, c in peers
        ]
        for copy in copies:
            copy.start()
        return copies

    column = [(0, c) for c in others]
    kept_copies = share(kept_rows.at[me], kept_rows.at[me], 0, everyone, all_send, all_recv)
    metric_copies = share(metrics.at[own], metrics.at[own], 0, column, near_send, near_recv)
    list_copies = share(lists.at[me_col], lists.at[me_col], 1, column, near_send, near_recv)
    panel_copies = share(panels.at[me], panels.at[me], 2, column, near_send, near_recv)
    for copy in kept_copies:
        copy.wait_recv()

    square = (LANES, LANES)
    down, across = lax.broadcasted_iota(i32, square, 0), lax.broadcasted_iota(i32, square, 1)
    kept = kept_rows[:, 0, :].astype(f32)
    if devices < LANES:
        kept = jnp.concatenate([kept, jnp.zeros((LANES - devices, LANES), f32)], axis=0)
    running = jnp.dot(kept.astype(bf16), (down <= across).astype(bf16), preferred_element_type=f32)
    ranks = jnp.where(kept > 0, running - 1.0, -256.0).astype(bf16)

    def place(panel_of, count):
        row_id = lax.broadcasted_iota(i32, (count, LANES), 0)
        col_id = lax.broadcasted_iota(i32, (count, LANES), 1)
        real = (row_id % PLACES < listed) & (row_id < cols * PLACES)
        hot = ((panel_of == col_id) & real).astype(bf16)
        counts = jnp.sum(jnp.dot(hot, kept.astype(bf16), preferred_element_type=f32), axis=1, keepdims=True)
        before = lax.broadcasted_iota(i32, (count, count), 1)
        after = lax.broadcasted_iota(i32, (count, count), 0)
        ahead = ((after // PLACES == before // PLACES) & (before < after)).astype(bf16)
        starts = jnp.dot(
            ahead, jnp.broadcast_to(counts, (count, LANES)).astype(bf16), preferred_element_type=f32)
        rank = jnp.dot(hot, ranks, preferred_element_type=f32)
        spots = jnp.where(real & (rank >= 0) & (col_id < block_size), rank + starts, -1.0)
        return spots, jnp.sum(counts, axis=0, keepdims=True)

    spots, kept_here = place(lists[me_col, :, block_size : block_size + 1], PLACES)
    places[:PLACES, :] = spots
    totals[me] = jnp.broadcast_to(kept_here.astype(i32), (1, LANES))

    def choose(e, carry):
        spot = jnp.broadcast_to(places[pl.ds(e, 1), :], (block_size, LANES))
        half = lax.broadcasted_iota(i32, (block_size, LANES), 1)
        spot = jnp.sum(
            jnp.where(lax.broadcasted_iota(i32, (block_size, LANES), 0) == half, spot, 0.0), axis=1, keepdims=True)
        for t in range(tiles):
            pick[t, e] = (spot == (half + t * LANES).astype(f32)).astype(f32).astype(bf16)
        return carry

    lax.fori_loop(0, listed, choose, 0)

    for copy in metric_copies:
        copy.wait_recv()
    for e in range(listed):
        chosen[e] = lax.dot_general(
            order, metrics[slot_ref[list_ref[2, e]]], (((1,), (1,)), ((), ())),
            preferred_element_type=f32).astype(bf16)

    left_half = lax.broadcasted_iota(i32, (block_size, LANES), 1) < block_size

    def apply(pair, carry):
        for h in range(2):
            e = pair * 2 + h
            pltpu.make_async_copy(integrals_ref.at[e], blocks.at[e], loads.at[e]).wait()
        for j in range(lines // 2):
            both = [
                jnp.dot(
                    chosen[pair * 2 + h], blocks[pair * 2 + h, :, 2 * j * LANES : 2 * (j + 1) * LANES],
                    preferred_element_type=f32)
                for h in range(2)
            ]
            for half in range(2):
                a, b = (value[:, half * LANES : (half + 1) * LANES] for value in both)
                parts = (
                    jnp.where(left_half, a, pltpu.roll(b, block_size, 1)).astype(bf16),
                    jnp.where(left_half, pltpu.roll(a, block_size, 1), b).astype(bf16),
                )
                line = 2 * j + half
                for odd in range(2):
                    for p in range(phases):
                        made[p, pair, odd, line * 16 : (line + 1) * 16, :] = parts[odd][p * 16 : (p + 1) * 16, :]
        return carry

    lax.fori_loop(0, listed // 4, apply, 0)
    for copy in panel_copies:
        copy.wait_recv()
    group = pl.ds(me_row * cols, cols)
    row_copies = share(
        panels.at[group], panels.at[group], 0, [(r, 0) for r in range(rows - 1, 0, -1)], row_send, row_recv)
    lax.fori_loop(listed // 4, listed // 2, apply, 0)

    def pack(p, carry):
        def columns(odd, inner):
            left = jnp.concatenate([made[p, pair, odd] for pair in range(listed // 2)], axis=1)
            for t in range(0, tiles, 2):
                width = min(2, tiles - t)
                right = jnp.concatenate(
                    [pick[t + k].reshape(listed * block_size, LANES) for k in range(width)], axis=1)
                value = jnp.dot(left, right, preferred_element_type=f32)
                for line in range(lines):
                    for g in range(2):
                        for k in range(width):
                            turned[t + k, pl.ds(g * 8 * lines + line, 8, stride=lines), :] = value[
                                line * 16 + g * 8 : line * 16 + g * 8 + 8, k * LANES : (k + 1) * LANES]
            for c in range(cols):
                for i in range(DEPTH):
                    row = (c * DEPTH + i) * lines
                    leaving[p, odd, c, i] = turned[:, row : row + lines, :].astype(bf16)
            for d in others:
                pltpu.make_async_remote_copy(
                    leaving.at[p, odd, lax.bitwise_xor(me_col, d)], arriving.at[p, odd, me_col],
                    sends.at[p, odd, d], recvs.at[p, odd, d], device_id=peer(0, d), device_id_type=MESH).start()
            arriving[p, odd, me_col] = leaving[p, odd, me_col]
            return inner

        lax.fori_loop(0, 2, columns, 0)
        return carry

    lax.fori_loop(0, phases, pack, 0)
    total_copies = share(totals.at[me], totals.at[me], 1, everyone, all_send, all_recv)
    for copy in list_copies:
        copy.wait_recv()
    mine = lists[...].reshape(cols * PLACES, LANES)
    if cols * PLACES < LANES:
        mine = jnp.concatenate([mine, jnp.full((LANES - cols * PLACES, LANES), 4 * LANES, i32)], axis=0)
    key = mine[:, 0:1]
    panel_of = mine[:, block_size : block_size + 1]
    places[...] = place(panel_of, LANES)[0]

    key_down = jnp.broadcast_to(key, square)
    key_across = jnp.broadcast_to(
        jnp.sum(jnp.where(down == across, key_down, 0), axis=0, keepdims=True), square)
    same_before = jnp.where((key_down == key_across) & (across < down), 1, 0)
    before = jnp.where(key_across < key_down, 1, 0) + same_before
    position = jnp.sum(before, axis=1, keepdims=True)
    repeats = jnp.minimum(jnp.sum(same_before, axis=1, keepdims=True), 1)
    at = position == across
    compact = down // PLACES * listed + down % PLACES
    table[0:1, :] = jnp.sum(jnp.where(at, compact, 0), axis=0, keepdims=True)
    table[1:2, :] = jnp.sum(jnp.where(at, repeats, 0), axis=0, keepdims=True)
    upto = jnp.sum(jnp.where(key_down <= across, 1, 0), axis=0, keepdims=True) - 1
    present = jnp.sum(jnp.where(key_down == across, 1, 0), axis=0, keepdims=True)
    table[2:3, :] = jnp.where(present > 0, upto, cols * listed)
    table[3:4, :] = jnp.sum(jnp.where(down == across, panel_of, 0), axis=0, keepdims=True)
    table[4:8, :] = jnp.zeros((4, LANES), i32)
    down_table = pltpu.make_async_copy(table, entry, moved)
    down_table.start()

    halves[cols * listed] = jnp.zeros((DEPTH, block_size, LANES), bf16)
    for a in range(2):
        tile[a * (side // 2) : (a + 1) * (side // 2), :] = jnp.zeros((side // 2, side), f32)
    down_table.wait()
    for copy in row_copies:
        copy.wait_recv()

    def gather(at_pair, carry):
        c, pair = at_pair // (listed // 2), at_pair % (listed // 2)
        for h in range(2):
            place = c * PLACES + pair * 2 + h
            spot = jnp.broadcast_to(places[pl.ds(place, 1), :][:, :block_size], (cap, block_size))
            chosen_rows = (spot == lax.broadcasted_iota(i32, (cap, block_size), 0).astype(f32)).astype(f32).astype(bf16)
            packed[c, pair, :, h * LANES : (h + 1) * LANES] = jnp.dot(
                chosen_rows, panels[entry[3, place]], preferred_element_type=f32).astype(bf16)
        return carry

    lax.fori_loop(0, cols * (listed // 2), gather, 0)

    def phase(p, carry):
        def source(d, inner):
            c = lax.bitwise_xor(me_col, d)

            @pl.when(d > 0)
            def _():
                for odd in range(2):
                    pltpu.make_async_remote_copy(
                        leaving.at[p, odd, c], arriving.at[p, odd, c], sends.at[p, odd, d], recvs.at[p, odd, d],
                        device_id=(me_row, c), device_id_type=MESH).wait_recv()

            left = jnp.concatenate(
                [
                    jnp.concatenate([arriving[p, odd, c, i, t] for t in range(tiles)], axis=1)
                    for odd in range(2)
                    for i in range(DEPTH)
                ],
                axis=0,
            )
            for pair in range(listed // 2):
                value = jnp.dot(left, packed[c, pair], preferred_element_type=f32)
                for h in range(2):
                    for odd in range(2):
                        for i in range(DEPTH):
                            row = (odd * DEPTH + i) * lines
                            terms[c * listed + pair * 2 + h, i, pl.ds(odd, lines, stride=2), :] = value[row : row + lines, h * LANES : (h + 1) * LANES]
            return inner

        lax.fori_loop(0, cols, source, 0)

        def segment(r, total):
            for k in range(4):
                at = r * 4 + k
                again = entry[1, at].astype(f32)
                total = terms[entry[0, at]] + total * again
                halves[at] = total.astype(bf16)
            return total

        lax.fori_loop(0, cols * listed // 4, segment, jnp.zeros((DEPTH, block_size, LANES), f32))

        def products(s, inner):
            strip = []
            for a in range(MB):
                parts = []
                for k in range(BATCH):
                    cell = halves[entry[2, (s * BATCH + k) * MB + a]]
                    parts.extend(cell[i] for i in range(DEPTH))
                strip.append(jnp.concatenate(parts, axis=1))
            high = jnp.concatenate(strip[: MB // 2], axis=0)
            low = jnp.concatenate(strip[MB // 2 :], axis=0)
            half = side // 2
            for left, right, a, b in ((high, high, 0, 0), (high, low, 0, 1), (low, low, 1, 1)):
                tile[a * half : (a + 1) * half, b * half : (b + 1) * half] += lax.dot_general(
                    left, right, (((1,), (1,)), ((), ())), preferred_element_type=f32)
            return inner

        lax.fori_loop(0, slots // BATCH, products, 0)
        return carry

    lax.fori_loop(0, phases, phase, 0)
    half = side // 2
    tile[half:, :half] = tile[:half, half:].T

    scale = 1.0 / (slots * block_size * LANES)
    share = out_ref.shape[0]
    middle = cols // 2
    opposite = lax.bitwise_xor(me_col, middle)

    def rows_of(col):
        return pl.ds(pl.multiple_of(col * share, share), share)

    strips = [pl.ds(q * (side // 2), side // 2) for q in range(2)]
    near = {}
    for far_side, q in ((1, 0), (1, 1), (0, 0), (0, 1)):
        for d in range(1, middle):
            target = lax.bitwise_xor(me_col, d)
            near[far_side, q, d] = pltpu.make_async_remote_copy(
                tile.at[rows_of(lax.bitwise_xor(target, far_side * middle)), strips[q]],
                landed.at[far_side, d - 1, :, strips[q]],
                red_send.at[far_side, q, d], red_recv.at[far_side, q, d],
                device_id=(me_row, target), device_id_type=MESH)
            near[far_side, q, d].start()
    far = []
    for q in range(2):
        total = tile[rows_of(opposite), strips[q]]
        for d in range(1, middle):
            near[1, q, d].wait_recv()
            total = total + landed[1, d - 1, :, strips[q]]
        crossing[q] = total
        far.append(pltpu.make_async_remote_copy(
            crossing.at[q], crossed.at[q], red_send.at[0, q, 0], red_recv.at[0, q, 0],
            device_id=(me_row, opposite), device_id_type=MESH))
        far[-1].start()
    for copy in total_copies:
        copy.wait_recv()
    table[0:1, :] = jnp.max(totals[:, 0, :], axis=0, keepdims=True)
    verdict = pltpu.make_async_copy(table, entry, moved)
    verdict.start()
    for q in range(2):
        total = tile[rows_of(me_col), strips[q]]
        for d in range(1, middle):
            near[0, q, d].wait_recv()
            total = total + landed[0, d - 1, :, strips[q]]
        far[q].wait_recv()
        out_ref[:, strips[q]] = (total + crossed[q]) * scale
    verdict.wait()
    flag_ref[0] = (entry[0, 0] <= cap).astype(i32)
    copies = metric_copies + kept_copies + list_copies + panel_copies + row_copies + total_copies
    for copy in copies + list(near.values()) + far:
        copy.wait_send()

    def finish(p, carry):
        for d in others:
            c = lax.bitwise_xor(me_col, d)
            for odd in range(2):
                pltpu.make_async_remote_copy(
                    leaving.at[p, odd, c], arriving.at[p, odd, me_col], sends.at[p, odd, d], recvs.at[p, odd, d],
                    device_id=(me_row, c), device_id_type=MESH).wait_send()
        return carry

    lax.fori_loop(0, phases, finish, 0)


def fused(integrals, block_list, p_slot, metric, density_panel, pattern):
    rows, cols = lax.axis_size("row"), lax.axis_size("col")
    listed, block_size, flat = integrals.shape
    slots = metric.shape[0] * cols
    devices = rows * cols
    side = MB * block_size
    lines = flat // LANES
    phases = block_size // (cols * DEPTH)
    cap = -(-(listed * block_size * 5 // 6) // LANES) * LANES
    tiles = cap // LANES
    bf16, f32, i32 = jnp.bfloat16, jnp.float32, jnp.int32
    half = cols // 2
    dma = pltpu.SemaphoreType.DMA
    out, flag = pl.pallas_call(
        functools.partial(fused_kernel, rows, cols, cap),
        out_shape=(
            jax.ShapeDtypeStruct((side // cols, side), f32),
            jax.ShapeDtypeStruct((1,), i32),
        ),
        in_specs=[ANY] * 6,
        out_specs=(VMEM, SMEM),
        scratch_shapes=[
            pltpu.SMEM((3, listed), i32),
            pltpu.SMEM(p_slot.shape, i32),
            pltpu.VMEM((1, block_size), i32),
            pltpu.VMEM(density_panel.shape, bf16),
            dma((5,)),
            pltpu.VMEM((devices, 1, LANES), i32),
            pltpu.VMEM((devices, 1, LANES), i32),
            pltpu.VMEM((cols, PLACES, LANES), i32),
            pltpu.VMEM((slots, block_size, block_size), bf16),
            pltpu.VMEM((devices, block_size, LANES), bf16),
            pltpu.VMEM((listed, block_size, flat), bf16),
            pltpu.VMEM((listed, block_size, block_size), bf16),
            pltpu.VMEM((phases, listed // 2, 2, lines * 16, LANES), bf16),
            pltpu.VMEM((tiles, listed, block_size, LANES), bf16),
            pltpu.VMEM((tiles, 16 * lines, LANES), f32),
            pltpu.VMEM((phases, 2, cols, DEPTH, tiles, lines, LANES), bf16),
            pltpu.VMEM((phases, 2, cols, DEPTH, tiles, lines, LANES), bf16),
            pltpu.VMEM((LANES, LANES), f32),
            pltpu.VMEM((8, LANES), i32),
            pltpu.SMEM((8, LANES), i32),
            pltpu.VMEM((cols, listed // 2, cap, 2 * LANES), bf16),
            pltpu.VMEM((cols * listed, DEPTH, block_size, LANES), f32),
            pltpu.VMEM((cols * listed + 1, DEPTH, block_size, LANES), bf16),
            pltpu.VMEM((side, side), f32),
            pltpu.VMEM((2, half - 1, side // cols, side), f32),
            pltpu.VMEM((2, side // cols, side // 2), f32),
            pltpu.VMEM((2, side // cols, side // 2), f32),
            dma((listed,)),
            dma((3, cols)),
            dma((3, cols)),
            dma((1, devices)),
            dma((1, devices)),
            dma((2, devices)),
            dma((2, devices)),
            dma((phases, 2, cols)),
            dma((phases, 2, cols)),
            dma((2, 2, half)),
            dma((2, 2, half)),
            dma,
        ],
        compiler_params=pltpu.CompilerParams(
            collective_id=3, has_side_effects=True, vmem_limit_bytes=63 * 2**20),
        name="fused",
    )(block_list.T, p_slot, pattern.reshape(1, -1), density_panel, metric, integrals)
    return out, flag


def on_device(integrals, block_list, p_slot, metric, density_panel, pattern):
    arguments = (integrals, block_list, p_slot, metric, density_panel, pattern)
    listed, block_size, flat = integrals.shape
    if not shapes_allow(
        lax.axis_size("row"), lax.axis_size("col"), listed, block_size, metric.shape[0],
        density_panel.shape[0], density_panel.shape[1], flat,
    ):
        return in_phases(*arguments)
    out, flag = fused(*arguments)
    return lax.cond(flag[0] > 0, lambda *_: out, in_phases, *arguments)


def solution(mesh):
    placed = (
        P(("row", "col"), None, None),
        P(("row", "col"), None),
        P(),
        P("col", None, None),
        P(("row", "col"), None),
        P(("row", "col")),
    )
    return jax.shard_map(
        on_device, mesh=mesh, in_specs=placed, out_specs=P(("row", "col"), None), check_vma=False
    )
```

```python
import functools

import jax
import jax.numpy as jnp
from jax import lax
from jax.experimental import pallas as pl
from jax.experimental.pallas import tpu as pltpu
from jax.sharding import PartitionSpec as P

MB = 8
LANES = 128
DEPTH = 2
PLACES = 16
BATCH = 4
MESH = pl.DeviceIdType.MESH
ANY = pl.BlockSpec(memory_space=pl.ANY)
VMEM = pl.BlockSpec(memory_space=pltpu.VMEM)
SMEM = pl.BlockSpec(memory_space=pltpu.SMEM)


def spread_kernel(axis, count, *refs):
    sources, targets = refs[:count], refs[count : 2 * count]
    sends, recvs, local = refs[2 * count :]
    me = lax.axis_index(axis)
    others = range(1, lax.axis_size(axis))

    def device(b):
        return {axis: lax.bitwise_xor(me, b)}

    barrier = pltpu.get_barrier_semaphore()
    for b in others:
        pl.semaphore_signal(barrier, inc=1, device_id=device(b), device_id_type=MESH)
    own = [
        pltpu.make_async_copy(source, target.at[me], local.at[k])
        for k, (source, target) in enumerate(zip(sources, targets))
    ]
    for copy in own:
        copy.start()
    pl.semaphore_wait(barrier, len(others))
    copies = []
    for k, (source, target) in enumerate(zip(sources, targets)):
        for b in others:
            copies.append(pltpu.make_async_remote_copy(
                source, target.at[me], sends.at[k, b], recvs.at[k, b],
                device_id=device(b), device_id_type=MESH))
            copies[-1].start()
    for copy in own + copies:
        copy.wait()


def spread(axis, size, number, arrays):
    count = len(arrays)
    return pl.pallas_call(
        functools.partial(spread_kernel, axis, count),
        out_shape=tuple(jax.ShapeDtypeStruct((size,) + a.shape, a.dtype) for a in arrays),
        in_specs=[VMEM] * count,
        out_specs=(VMEM,) * count,
        scratch_shapes=[
            pltpu.SemaphoreType.DMA((count, size)),
            pltpu.SemaphoreType.DMA((count, size)),
            pltpu.SemaphoreType.DMA((count,)),
        ],
        compiler_params=pltpu.CompilerParams(collective_id=number, has_side_effects=True),
        name="spread_" + axis,
    )(*arrays)


def apply_kernel(cols, depth, slot_ref, pick_ref, metric_ref, block_ref, *refs):
    outs, chosen, turned = refs[:cols], refs[cols], refs[cols + 1]
    lines = block_ref.shape[2] // LANES
    here = block_ref.shape[0]

    @pl.when(pl.program_id(0) == 0)
    def _():
        for e in range(chosen.shape[0]):
            chosen[e] = lax.dot_general(
                pick_ref[...], metric_ref[slot_ref[e]], (((1,), (1,)), ((), ())),
                preferred_element_type=jnp.float32).astype(jnp.bfloat16)

    for k in range(here):
        made = jnp.dot(
            chosen[pl.program_id(0) * here + k], block_ref[k], preferred_element_type=jnp.float32)
        total = made.shape[0]
        for start in range(0, total, 8):
            size = min(8, total - start)
            for line in range(lines):
                turned[k, pl.ds(start * lines + line, size, stride=lines), :] = made[
                    start : start + size, line * LANES : (line + 1) * LANES]
        for d in range(cols):
            for i in range(depth):
                row = (d * depth + i) * lines
                outs[d][i, k] = turned[k, row : row + lines, :].astype(jnp.bfloat16)


def apply_metric(cols, slot_ids, pick, metrics, integrals):
    listed, block_size, flat = integrals.shape
    lines = flat // LANES
    depth = pick.shape[0] // cols
    here = 3 if listed % 3 == 0 else 1
    shape = jax.ShapeDtypeStruct((depth, listed, lines, LANES), jnp.bfloat16)
    return pl.pallas_call(
        functools.partial(apply_kernel, cols, depth),
        grid=(listed // here,),
        out_shape=(shape,) * cols,
        in_specs=[SMEM, VMEM, VMEM, pl.BlockSpec((here, block_size, flat), lambda e: (e, 0, 0))],
        out_specs=(pl.BlockSpec((depth, here, lines, LANES), lambda e: (0, e, 0, 0)),) * cols,
        scratch_shapes=[
            pltpu.VMEM((listed, cols * depth, block_size), jnp.bfloat16),
            pltpu.VMEM((here, cols * depth * lines, LANES), jnp.float32),
        ],
        cost_estimate=pl.CostEstimate(flops=10**9, bytes_accessed=8 * 2**20, transcendentals=0),
        name="apply_metric",
    )(slot_ids, pick, metrics, integrals)


def build_kernel(cols, sizes, first, scale, corner_ref, second_ref, panel_ref, tile_ref, *refs):
    chunks, out_ref, acc = refs[:cols], refs[cols], refs[cols + 1]
    slots, side, block_size = sizes
    depth, listed, lines, _ = chunks[0].shape
    parity = LANES // block_size
    step = 6 if listed % 6 == 0 else 1
    acc[...] = jnp.zeros_like(acc)
    for d in range(cols):
        def entries(at, carry, d=d):
            made = []
            for k in range(step):
                e = at * step + k
                rows = chunks[d][:, pl.ds(e, 1)].reshape(depth * lines, LANES)
                made.append(jnp.dot(
                    rows, panel_ref[second_ref[d * listed + e]], preferred_element_type=jnp.float32))
            for k in range(step):
                corner = corner_ref[d * listed + at * step + k]
                for i in range(depth):
                    for odd in range(parity):
                        where = pl.ds(corner + odd, lines, stride=parity)
                        acc[i, where, :] += made[k][
                            i * lines : (i + 1) * lines, odd * LANES : (odd + 1) * LANES]
            return carry

        lax.fori_loop(0, listed // step, entries, 0)

    half = side // 2
    corners = ((0, 0), (0, 1), (1, 1))
    for a, b in corners:
        at = (slice(a * half, (a + 1) * half), slice(b * half, (b + 1) * half))
        out_ref[at] = jnp.zeros((half, half), jnp.float32) if first else tile_ref[at]
    batch = 4

    def products(group, carry):
        wide = jnp.concatenate(
            [
                acc[i, pl.ds(pl.multiple_of((group * batch + k) * side, side), side), :].astype(jnp.bfloat16)
                for k in range(batch)
                for i in range(depth)
            ],
            axis=1,
        )
        for a, b in corners:
            at = (slice(a * half, (a + 1) * half), slice(b * half, (b + 1) * half))
            out_ref[at] += lax.dot_general(
                wide[a * half : (a + 1) * half], wide[b * half : (b + 1) * half],
                (((1,), (1,)), ((), ())), preferred_element_type=jnp.float32)
        return carry

    lax.fori_loop(0, slots // batch, products, 0)
    if scale is not None:
        for a, b in corners:
            at = (slice(a * half, (a + 1) * half), slice(b * half, (b + 1) * half))
            out_ref[at] = out_ref[at] * scale
        out_ref[half:, :half] = out_ref[:half, half:].T


def build(cols, sizes, first, scale, corner, second, panels, tile, chunks):
    slots, side, _ = sizes
    depth = chunks[0].shape[0]
    return pl.pallas_call(
        functools.partial(build_kernel, cols, sizes, first, scale),
        out_shape=jax.ShapeDtypeStruct((side, side), jnp.float32),
        in_specs=[SMEM, SMEM, VMEM, VMEM] + [VMEM] * cols,
        out_specs=VMEM,
        scratch_shapes=[pltpu.VMEM((depth, slots * side, LANES), jnp.float32)],
        compiler_params=pltpu.CompilerParams(vmem_limit_bytes=56 * 2**20),
        cost_estimate=pl.CostEstimate(flops=10**10, bytes_accessed=8 * 2**20, transcendentals=0),
        name="build_tile",
    )(corner, second, panels, tile, *chunks)


def reduce_kernel(cols, tile_ref, out_ref, landed, crossing, crossed, sends, recvs):
    me_row, me_col = lax.axis_index("row"), lax.axis_index("col")
    share = out_ref.shape[0]
    half = cols // 2
    opposite = lax.bitwise_xor(me_col, half)

    def rows_of(col):
        return pl.ds(pl.multiple_of(col * share, share), share)

    barrier = pltpu.get_barrier_semaphore()
    for d in range(1, half + 1):
        pl.semaphore_signal(
            barrier, inc=1, device_id=(me_row, lax.bitwise_xor(me_col, d)), device_id_type=MESH)
    pl.semaphore_wait(barrier, half)
    near = []
    for side in (1, 0):
        for d in range(1, half):
            peer = lax.bitwise_xor(me_col, d)
            near.append(pltpu.make_async_remote_copy(
                tile_ref.at[rows_of(lax.bitwise_xor(peer, side * half))], landed.at[side, d - 1],
                sends.at[side, d - 1], recvs.at[side, d - 1], device_id=(me_row, peer), device_id_type=MESH))
            near[-1].start()
    total = tile_ref[rows_of(opposite), :]
    for d in range(1, half):
        near[d - 1].wait_recv()
        total = total + landed[1, d - 1]
    crossing[...] = total
    total = tile_ref[rows_of(me_col), :]
    out_ref[...] = total
    far = pltpu.make_async_remote_copy(
        crossing, crossed, sends.at[0, half - 1], recvs.at[0, half - 1],
        device_id=(me_row, opposite), device_id_type=MESH)
    far.start()
    for d in range(1, half):
        near[half - 2 + d].wait_recv()
        total = total + landed[0, d - 1]
    far.wait_recv()
    out_ref[...] = total + crossed[...]
    for copy in near:
        copy.wait_send()
    far.wait_send()


def reduce_tiles(cols, tile):
    side = tile.shape[0]
    half = cols // 2
    return pl.pallas_call(
        functools.partial(reduce_kernel, cols),
        out_shape=jax.ShapeDtypeStruct((side // cols, side), jnp.float32),
        in_specs=[VMEM],
        out_specs=VMEM,
        scratch_shapes=[
            pltpu.VMEM((2, half - 1, side // cols, side), jnp.float32),
            pltpu.VMEM((side // cols, side), jnp.float32),
            pltpu.VMEM((side // cols, side), jnp.float32),
            pltpu.SemaphoreType.DMA((2, half)),
            pltpu.SemaphoreType.DMA((2, half)),
        ],
        compiler_params=pltpu.CompilerParams(collective_id=1, has_side_effects=True),
        name="reduce_tiles",
    )(tile)


def in_phases(integrals, block_list, p_slot, metric, density_panel, pattern):
    rows, cols = lax.axis_size("row"), lax.axis_size("col")
    me_col = lax.axis_index("col")
    owned_slots, block_size = metric.shape[0], metric.shape[1]
    listed = integrals.shape[0]
    panel_width = density_panel.shape[1]
    slots = owned_slots * cols
    side = MB * block_size
    mine = block_size // cols
    depth = DEPTH if mine % DEPTH == 0 else 1
    phases = mine // depth
    metrics, panels_col, patterns_col, lists_col = spread(
        "col", cols, 0, (metric, density_panel, pattern.reshape(1, -1), block_list))
    metrics = metrics.reshape(slots, block_size, block_size)
    slot_match = block_list[:, 2][:, None] == jnp.arange(slots, dtype=jnp.int32)[None, :]
    slot_ids = jnp.sum(jnp.where(slot_match, p_slot[None, :], 0), axis=1)

    offsets = jnp.arange(cols, dtype=jnp.int32)
    peers = lax.bitwise_xor(offsets, me_col)
    places = jnp.arange(block_size, dtype=jnp.int32)
    sent = []
    for phase in range(phases):
        wanted = (peers[:, None] * mine + phase * depth + jnp.arange(depth, dtype=jnp.int32)).reshape(-1)
        pick = (wanted[:, None] == places[None, :]).astype(jnp.bfloat16)
        outgoing = apply_metric(cols, slot_ids, pick, metrics, integrals)
        arrived = [outgoing[0]]
        for d in range(1, cols):
            arrived.append(lax.ppermute(outgoing[d], "col", [(c, c ^ d) for c in range(cols)]))
        sent.append(arrived)
        if phase == 0:
            panels_col, patterns_col, lists_col, _ = lax.optimization_barrier(
                (panels_col, patterns_col, lists_col, outgoing[1]))

    panel_all, pattern_all = spread("row", rows, 2, (panels_col, patterns_col))
    panel_all = panel_all.reshape(-1, panel_width)
    panel_all = jnp.where(pattern_all.reshape(-1, 1) > 0, panel_all, jnp.zeros_like(panel_all))
    lists_in = jnp.sum(
        jnp.where((peers[:, None] == offsets[None, :])[:, :, None, None], lists_col[None], 0), axis=1)
    lists_in = lists_in.reshape(cols * listed, 3)
    match_in = lists_in[:, 2][:, None] == jnp.arange(slots, dtype=jnp.int32)[None, :]
    slots_in = jnp.sum(jnp.where(match_in, p_slot[None, :], 0), axis=1)
    corner = slots_in * side + (lists_in[:, 0] - lax.axis_index("row") * MB) * block_size
    second = lists_in[:, 1]
    parity = LANES // block_size
    blocks = panel_all.reshape(-1, block_size, panel_width)
    panels = jnp.concatenate(
        [
            jnp.pad(blocks, ((0, 0), (0, 0), (k * panel_width, (parity - 1 - k) * panel_width)))
            for k in range(parity)
        ],
        axis=1,
    )
    tile = jnp.zeros((8, LANES), jnp.float32)
    for phase in range(phases):
        last = phase == phases - 1
        scale = 1.0 / (slots * block_size * panel_width) if last else None
        tile = build(
            cols, (slots, side, block_size), phase == 0, scale, corner, second, panels, tile, sent[phase])
    return reduce_tiles(cols, tile)


def shapes_allow(rows, cols, listed, block_size, owned_slots, local_rows, panel_width, flat):
    slots = owned_slots * cols
    return (
        listed <= PLACES
        and listed % 4 == 0
        and cols * PLACES <= LANES
        and slots * MB <= LANES
        and slots % BATCH == 0
        and local_rows == block_size
        and rows * cols <= LANES
        and 2 * block_size == LANES
        and panel_width == LANES
        and flat == block_size * block_size
        and block_size % (cols * DEPTH) == 0
        and cols * DEPTH == 16
    )


def fused_kernel(rows, cols, cap, list_in, slot_in, pattern_in, density_in, metric_in, integrals_ref,
                 out_ref, flag_ref, list_ref, slot_ref, pattern_ref, density_ref, inputs, kept_rows, totals, lists, metrics, panels, blocks, chosen, made, pick, turned,
                 leaving, arriving, places, table, entry, packed, terms, halves, tile, landed, crossing, crossed,
                 loads, near_send, near_recv, row_send, row_recv, all_send, all_recv, sends, recvs, red_send,
                 red_recv, moved):
    f32, bf16, i32 = jnp.float32, jnp.bfloat16, jnp.int32
    me_row, me_col = lax.axis_index("row"), lax.axis_index("col")
    me = me_row * cols + me_col
    listed, block_size, flat = blocks.shape
    slots = metrics.shape[0]
    owned = slots // cols
    lines = flat // LANES
    phases = block_size // (cols * DEPTH)
    devices = rows * cols
    tiles = cap // LANES
    side = MB * block_size
    others = tuple(range(cols // 2, cols)) + tuple(range(1, cols // 2))
    everyone = [(r, c) for c in others + (0,) for r in range(rows) if r or c]

    def peer(r, c):
        return (lax.bitwise_xor(me_row, r), lax.bitwise_xor(me_col, c))

    barrier = pltpu.get_barrier_semaphore()
    for r, c in everyone:
        pl.semaphore_signal(barrier, inc=1, device_id=peer(r, c), device_id_type=MESH)
    own = pl.ds(me_col * owned, owned)
    small = [
        pltpu.make_async_copy(source, target, inputs.at[k])
        for k, (source, target) in enumerate((
            (pattern_in, pattern_ref),
            (list_in, list_ref),
            (slot_in, slot_ref),
            (metric_in, metrics.at[own]),
            (density_in, density_ref),
        ))
    ]
    fetches = [pltpu.make_async_copy(integrals_ref.at[e], blocks.at[e], loads.at[e]) for e in range(listed)]
    for fetch in small + fetches:
        fetch.start()
    for fetch in small:
        fetch.wait()

    lane = lax.broadcasted_iota(i32, (1, LANES), 1)
    for e in range(PLACES):
        if e < listed:
            key = slot_ref[list_ref[2, e]] * MB + list_ref[0, e] - me_row * MB
            lists[me_col, e : e + 1, :] = jnp.where(lane < block_size, key, list_ref[1, e])
        else:
            lists[me_col, e : e + 1, :] = jnp.where(lane < block_size, 4 * LANES, 0)
    pattern = (pattern_ref[...] > 0).astype(i32)
    kept_rows[me] = jnp.concatenate([pattern, jnp.zeros_like(pattern)], axis=1)
    eye = lax.broadcasted_iota(i32, (block_size, block_size), 0) == lax.broadcasted_iota(
        i32, (block_size, block_size), 1)
    keep = jnp.sum(
        jnp.where(eye, jnp.broadcast_to(pattern.astype(f32), (block_size, block_size)), 0.0), axis=1, keepdims=True)
    panels[me] = jnp.where(keep > 0, density_ref[...].astype(f32), 0.0).astype(bf16)
    wanted = lax.broadcasted_iota(i32, (block_size, block_size), 0)
    wanted = (wanted // DEPTH % cols) * (block_size // cols) + wanted // (cols * DEPTH) * DEPTH + wanted % DEPTH
    order = (wanted == lax.broadcasted_iota(i32, (block_size, block_size), 1)).astype(bf16)

    pl.semaphore_wait(barrier, devices - 1)

    def share(ref, target, k, peers, send_sems, recv_sems):
        copies = [
            pltpu.make_async_remote_copy(
                ref, target, send_sems.at[k, r * cols + c], recv_sems.at[k, r * cols + c],
                device_id=peer(r, c), device_id_type=MESH)
            for r, c in peers
        ]
        for copy in copies:
            copy.start()
        return copies

    column = [(0, c) for c in others]
    kept_copies = share(kept_rows.at[me], kept_rows.at[me], 0, everyone, all_send, all_recv)
    metric_copies = share(metrics.at[own], metrics.at[own], 0, column, near_send, near_recv)
    list_copies = share(lists.at[me_col], lists.at[me_col], 1, column, near_send, near_recv)
    panel_copies = share(panels.at[me], panels.at[me], 2, column, near_send, near_recv)
    for copy in kept_copies:
        copy.wait_recv()

    square = (LANES, LANES)
    down, across = lax.broadcasted_iota(i32, square, 0), lax.broadcasted_iota(i32, square, 1)
    kept = kept_rows[:, 0, :].astype(f32)
    if devices < LANES:
        kept = jnp.concatenate([kept, jnp.zeros((LANES - devices, LANES), f32)], axis=0)
    running = jnp.dot(kept.astype(bf16), (down <= across).astype(bf16), preferred_element_type=f32)
    ranks = jnp.where(kept > 0, running - 1.0, -256.0).astype(bf16)

    def place(panel_of, count):
        row_id = lax.broadcasted_iota(i32, (count, LANES), 0)
        col_id = lax.broadcasted_iota(i32, (count, LANES), 1)
        real = (row_id % PLACES < listed) & (row_id < cols * PLACES)
        hot = ((panel_of == col_id) & real).astype(bf16)
        counts = jnp.sum(jnp.dot(hot, kept.astype(bf16), preferred_element_type=f32), axis=1, keepdims=True)
        before = lax.broadcasted_iota(i32, (count, count), 1)
        after = lax.broadcasted_iota(i32, (count, count), 0)
        ahead = ((after // PLACES == before // PLACES) & (before < after)).astype(bf16)
        starts = jnp.dot(
            ahead, jnp.broadcast_to(counts, (count, LANES)).astype(bf16), preferred_element_type=f32)
        rank = jnp.dot(hot, ranks, preferred_element_type=f32)
        spots = jnp.where(real & (rank >= 0) & (col_id < block_size), rank + starts, -1.0)
        return spots, jnp.sum(counts, axis=0, keepdims=True)

    spots, kept_here = place(lists[me_col, :, block_size : block_size + 1], PLACES)
    places[:PLACES, :] = spots
    totals[me] = jnp.broadcast_to(kept_here.astype(i32), (1, LANES))

    def choose(e, carry):
        spot = jnp.broadcast_to(places[pl.ds(e, 1), :], (block_size, LANES))
        half = lax.broadcasted_iota(i32, (block_size, LANES), 1)
        spot = jnp.sum(
            jnp.where(lax.broadcasted_iota(i32, (block_size, LANES), 0) == half, spot, 0.0), axis=1, keepdims=True)
        for t in range(tiles):
            pick[t, e] = (spot == (half + t * LANES).astype(f32)).astype(f32).astype(bf16)
        return carry

    lax.fori_loop(0, listed, choose, 0)

    for copy in metric_copies:
        copy.wait_recv()
    for e in range(listed):
        chosen[e] = lax.dot_general(
            order, metrics[slot_ref[list_ref[2, e]]], (((1,), (1,)), ((), ())),
            preferred_element_type=f32).astype(bf16)

    left_half = lax.broadcasted_iota(i32, (block_size, LANES), 1) < block_size

    def apply(pair, carry):
        for h in range(2):
            e = pair * 2 + h
            pltpu.make_async_copy(integrals_ref.at[e], blocks.at[e], loads.at[e]).wait()
        for j in range(lines // 2):
            both = [
                jnp.dot(
                    chosen[pair * 2 + h], blocks[pair * 2 + h, :, 2 * j * LANES : 2 * (j + 1) * LANES],
                    preferred_element_type=f32)
                for h in range(2)
            ]
            for half in range(2):
                a, b = (value[:, half * LANES : (half + 1) * LANES] for value in both)
                parts = (
                    jnp.where(left_half, a, pltpu.roll(b, block_size, 1)).astype(bf16),
                    jnp.where(left_half, pltpu.roll(a, block_size, 1), b).astype(bf16),
                )
                line = 2 * j + half
                for odd in range(2):
                    for p in range(phases):
                        made[p, pair, odd, line * 16 : (line + 1) * 16, :] = parts[odd][p * 16 : (p + 1) * 16, :]
        return carry

    lax.fori_loop(0, listed // 4, apply, 0)
    for copy in panel_copies:
        copy.wait_recv()
    group = pl.ds(me_row * cols, cols)
    row_copies = share(
        panels.at[group], panels.at[group], 0, [(r, 0) for r in range(rows - 1, 0, -1)], row_send, row_recv)
    lax.fori_loop(listed // 4, listed // 2, apply, 0)

    def passage(p, piece, k, d):
        c = lax.bitwise_xor(me_col, d)
        return pltpu.make_async_remote_copy(
            leaving.at[(p, c) + piece], arriving.at[(p, me_col) + piece], sends.at[p, k, d], recvs.at[p, k, d],
            device_id=(me_row, c), device_id_type=MESH)

    def by_parity(p, odd, d):
        return passage(p, (odd,), odd, d)

    def by_depth(p, i, d):
        return passage(p, (slice(None), i), i, d)

    def whole(p, d):
        return passage(p, (), 0, d)

    def pack(p, carry):
        def columns(odd, inner):
            left = jnp.concatenate([made[p, pair, odd] for pair in range(listed // 2)], axis=1)
            for t in range(0, tiles, 2):
                width = min(2, tiles - t)
                right = jnp.concatenate(
                    [pick[t + k].reshape(listed * block_size, LANES) for k in range(width)], axis=1)
                value = jnp.dot(left, right, preferred_element_type=f32)
                for line in range(lines):
                    for g in range(2):
                        for k in range(width):
                            turned[t + k, pl.ds(g * 8 * lines + line, 8, stride=lines), :] = value[
                                line * 16 + g * 8 : line * 16 + g * 8 + 8, k * LANES : (k + 1) * LANES]
            for c in range(cols):
                for i in range(DEPTH):
                    row = (c * DEPTH + i) * lines
                    leaving[p, c, odd, i] = turned[:, row : row + lines, :].astype(bf16)

            @pl.when(p == 0)
            def _():
                for d in others:
                    by_parity(p, odd, d).start()

            return inner

        lax.fori_loop(0, 2, columns, 0)

        @pl.when((p > 0) & (p < phases - 1))
        def _():
            for d in others:
                whole(p, d).start()

        @pl.when(p == phases - 1)
        def _():
            for i in range(DEPTH):
                for d in others:
                    by_depth(p, i, d).start()

        arriving[p, me_col] = leaving[p, me_col]
        return carry

    lax.fori_loop(0, phases, pack, 0)
    total_copies = share(totals.at[me], totals.at[me], 1, everyone, all_send, all_recv)
    for copy in list_copies:
        copy.wait_recv()
    mine = lists[...].reshape(cols * PLACES, LANES)
    if cols * PLACES < LANES:
        mine = jnp.concatenate([mine, jnp.full((LANES - cols * PLACES, LANES), 4 * LANES, i32)], axis=0)
    key = mine[:, 0:1]
    panel_of = mine[:, block_size : block_size + 1]
    places[...] = place(panel_of, LANES)[0]

    key_down = jnp.broadcast_to(key, square)
    key_across = jnp.broadcast_to(
        jnp.sum(jnp.where(down == across, key_down, 0), axis=0, keepdims=True), square)
    same_before = jnp.where((key_down == key_across) & (across < down), 1, 0)
    before = jnp.where(key_across < key_down, 1, 0) + same_before
    position = jnp.sum(before, axis=1, keepdims=True)
    repeats = jnp.minimum(jnp.sum(same_before, axis=1, keepdims=True), 1)
    at = position == across
    compact = down // PLACES * listed + down % PLACES
    table[0:1, :] = jnp.sum(jnp.where(at, compact, 0), axis=0, keepdims=True)
    table[1:2, :] = jnp.sum(jnp.where(at, repeats, 0), axis=0, keepdims=True)
    upto = jnp.sum(jnp.where(key_down <= across, 1, 0), axis=0, keepdims=True) - 1
    present = jnp.sum(jnp.where(key_down == across, 1, 0), axis=0, keepdims=True)
    table[2:3, :] = jnp.where(present > 0, upto, cols * listed)
    table[3:4, :] = jnp.sum(jnp.where(down == across, panel_of, 0), axis=0, keepdims=True)
    table[4:8, :] = jnp.zeros((4, LANES), i32)
    down_table = pltpu.make_async_copy(table, entry, moved)
    down_table.start()

    halves[cols * listed] = jnp.zeros((DEPTH, block_size, LANES), bf16)
    for a in range(2):
        tile[a * (side // 2) : (a + 1) * (side // 2), :] = jnp.zeros((side // 2, side), f32)
    down_table.wait()
    for copy in row_copies:
        copy.wait_recv()

    def gather(at_pair, carry):
        c, pair = at_pair // (listed // 2), at_pair % (listed // 2)
        for h in range(2):
            place = c * PLACES + pair * 2 + h
            spot = jnp.broadcast_to(places[pl.ds(place, 1), :][:, :block_size], (cap, block_size))
            chosen_rows = (spot == lax.broadcasted_iota(i32, (cap, block_size), 0).astype(f32)).astype(f32).astype(bf16)
            packed[c, pair, :, h * LANES : (h + 1) * LANES] = jnp.dot(
                chosen_rows, panels[entry[3, place]], preferred_element_type=f32).astype(bf16)
        return carry

    lax.fori_loop(0, cols * (listed // 2), gather, 0)

    def phase(p, first, count, arrived):
        def source(d, inner):
            c = lax.bitwise_xor(me_col, d)

            @pl.when(d > 0)
            def _():
                arrived(p, d)

            left = jnp.concatenate(
                [
                    jnp.concatenate([arriving[p, c, odd, first + i, t] for t in range(tiles)], axis=1)
                    for odd in range(2)
                    for i in range(count)
                ],
                axis=0,
            )
            for pair in range(listed // 2):
                value = jnp.dot(left, packed[c, pair], preferred_element_type=f32)
                for h in range(2):
                    for odd in range(2):
                        for i in range(count):
                            row = (odd * count + i) * lines
                            terms[c * listed + pair * 2 + h, i, pl.ds(odd, lines, stride=2), :] = value[
                                row : row + lines, h * LANES : (h + 1) * LANES]
            return inner

        lax.fori_loop(0, cols, source, 0)

        def segment(r, total):
            for k in range(4):
                at = r * 4 + k
                again = entry[1, at].astype(f32)
                total = terms[entry[0, at]][:count] + total * again
                halves[at, :count] = total.astype(bf16)
            return total

        lax.fori_loop(0, cols * listed // 4, segment, jnp.zeros((count, block_size, LANES), f32))

        def products(s, inner):
            strip = []
            for a in range(MB):
                parts = []
                for k in range(BATCH):
                    cell = halves[entry[2, (s * BATCH + k) * MB + a]]
                    parts.extend(cell[i] for i in range(count))
                strip.append(jnp.concatenate(parts, axis=1))
            high = jnp.concatenate(strip[: MB // 2], axis=0)
            low = jnp.concatenate(strip[MB // 2 :], axis=0)
            half = side // 2
            for left, right, a, b in ((high, high, 0, 0), (high, low, 0, 1), (low, low, 1, 1)):
                tile[a * half : (a + 1) * half, b * half : (b + 1) * half] += lax.dot_general(
                    left, right, (((1,), (1,)), ((), ())), preferred_element_type=f32)
            return inner

        lax.fori_loop(0, slots // BATCH, products, 0)

    def early(p, carry):
        def arrived(p, d):
            @pl.when(p == 0)
            def _():
                for odd in range(2):
                    by_parity(p, odd, d).wait_recv()

            @pl.when(p > 0)
            def _():
                whole(p, d).wait_recv()

        phase(p, 0, DEPTH, arrived)
        return carry

    lax.fori_loop(0, phases - 1, early, 0)

    def late(i, carry):
        phase(phases - 1, i, 1, lambda p, d: by_depth(p, i, d).wait_recv())
        return carry

    lax.fori_loop(0, DEPTH, late, 0)
    half = side // 2
    tile[half:, :half] = tile[:half, half:].T

    scale = 1.0 / (slots * block_size * LANES)
    share = out_ref.shape[0]
    middle = cols // 2
    opposite = lax.bitwise_xor(me_col, middle)

    def rows_of(col):
        return pl.ds(pl.multiple_of(col * share, share), share)

    strips = [pl.ds(q * (side // 2), side // 2) for q in range(2)]
    near = {}
    for far_side, q in ((1, 0), (1, 1), (0, 0), (0, 1)):
        for d in range(1, middle):
            target = lax.bitwise_xor(me_col, d)
            near[far_side, q, d] = pltpu.make_async_remote_copy(
                tile.at[rows_of(lax.bitwise_xor(target, far_side * middle)), strips[q]],
                landed.at[far_side, d - 1, :, strips[q]],
                red_send.at[far_side, q, d], red_recv.at[far_side, q, d],
                device_id=(me_row, target), device_id_type=MESH)
            near[far_side, q, d].start()
    far = []
    for q in range(2):
        total = tile[rows_of(opposite), strips[q]]
        for d in range(1, middle):
            near[1, q, d].wait_recv()
            total = total + landed[1, d - 1, :, strips[q]]
        crossing[q] = total
        far.append(pltpu.make_async_remote_copy(
            crossing.at[q], crossed.at[q], red_send.at[0, q, 0], red_recv.at[0, q, 0],
            device_id=(me_row, opposite), device_id_type=MESH))
        far[-1].start()
    for copy in total_copies:
        copy.wait_recv()
    table[0:1, :] = jnp.max(totals[:, 0, :], axis=0, keepdims=True)
    verdict = pltpu.make_async_copy(table, entry, moved)
    verdict.start()
    for q in range(2):
        total = tile[rows_of(me_col), strips[q]]
        for d in range(1, middle):
            near[0, q, d].wait_recv()
            total = total + landed[0, d - 1, :, strips[q]]
        far[q].wait_recv()
        out_ref[:, strips[q]] = (total + crossed[q]) * scale
    verdict.wait()
    flag_ref[0] = (entry[0, 0] <= cap).astype(i32)
    copies = metric_copies + kept_copies + list_copies + panel_copies + row_copies + total_copies
    for copy in copies + list(near.values()) + far:
        copy.wait_send()

    def finish(p, carry):
        for d in others:
            whole(p, d).wait_send()
        return carry

    lax.fori_loop(1, phases - 1, finish, 0)
    for d in others:
        for k in range(2):
            by_parity(0, k, d).wait_send()
            by_depth(phases - 1, k, d).wait_send()


def fused(integrals, block_list, p_slot, metric, density_panel, pattern):
    rows, cols = lax.axis_size("row"), lax.axis_size("col")
    listed, block_size, flat = integrals.shape
    slots = metric.shape[0] * cols
    devices = rows * cols
    side = MB * block_size
    lines = flat // LANES
    phases = block_size // (cols * DEPTH)
    cap = -(-(listed * block_size * 5 // 6) // LANES) * LANES
    tiles = cap // LANES
    bf16, f32, i32 = jnp.bfloat16, jnp.float32, jnp.int32
    half = cols // 2
    dma = pltpu.SemaphoreType.DMA
    out, flag = pl.pallas_call(
        functools.partial(fused_kernel, rows, cols, cap),
        out_shape=(
            jax.ShapeDtypeStruct((side // cols, side), f32),
            jax.ShapeDtypeStruct((1,), i32),
        ),
        in_specs=[ANY] * 6,
        out_specs=(VMEM, SMEM),
        scratch_shapes=[
            pltpu.SMEM((3, listed), i32),
            pltpu.SMEM(p_slot.shape, i32),
            pltpu.VMEM((1, block_size), i32),
            pltpu.VMEM(density_panel.shape, bf16),
            dma((5,)),
            pltpu.VMEM((devices, 1, LANES), i32),
            pltpu.VMEM((devices, 1, LANES), i32),
            pltpu.VMEM((cols, PLACES, LANES), i32),
            pltpu.VMEM((slots, block_size, block_size), bf16),
            pltpu.VMEM((devices, block_size, LANES), bf16),
            pltpu.VMEM((listed, block_size, flat), bf16),
            pltpu.VMEM((listed, block_size, block_size), bf16),
            pltpu.VMEM((phases, listed // 2, 2, lines * 16, LANES), bf16),
            pltpu.VMEM((tiles, listed, block_size, LANES), bf16),
            pltpu.VMEM((tiles, 16 * lines, LANES), f32),
            pltpu.VMEM((phases, cols, 2, DEPTH, tiles, lines, LANES), bf16),
            pltpu.VMEM((phases, cols, 2, DEPTH, tiles, lines, LANES), bf16),
            pltpu.VMEM((LANES, LANES), f32),
            pltpu.VMEM((8, LANES), i32),
            pltpu.SMEM((8, LANES), i32),
            pltpu.VMEM((cols, listed // 2, cap, 2 * LANES), bf16),
            pltpu.VMEM((cols * listed, DEPTH, block_size, LANES), f32),
            pltpu.VMEM((cols * listed + 1, DEPTH, block_size, LANES), bf16),
            pltpu.VMEM((side, side), f32),
            pltpu.VMEM((2, half - 1, side // cols, side), f32),
            pltpu.VMEM((2, side // cols, side // 2), f32),
            pltpu.VMEM((2, side // cols, side // 2), f32),
            dma((listed,)),
            dma((3, cols)),
            dma((3, cols)),
            dma((1, devices)),
            dma((1, devices)),
            dma((2, devices)),
            dma((2, devices)),
            dma((phases, 2, cols)),
            dma((phases, 2, cols)),
            dma((2, 2, half)),
            dma((2, 2, half)),
            dma,
        ],
        compiler_params=pltpu.CompilerParams(
            collective_id=3, has_side_effects=True, vmem_limit_bytes=63 * 2**20),
        name="fused",
    )(block_list.T, p_slot, pattern.reshape(1, -1), density_panel, metric, integrals)
    return out, flag


def on_device(integrals, block_list, p_slot, metric, density_panel, pattern):
    arguments = (integrals, block_list, p_slot, metric, density_panel, pattern)
    listed, block_size, flat = integrals.shape
    if not shapes_allow(
        lax.axis_size("row"), lax.axis_size("col"), listed, block_size, metric.shape[0],
        density_panel.shape[0], density_panel.shape[1], flat,
    ):
        return in_phases(*arguments)
    out, flag = fused(*arguments)
    return lax.cond(flag[0] > 0, lambda *_: out, in_phases, *arguments)


def solution(mesh):
    placed = (
        P(("row", "col"), None, None),
        P(("row", "col"), None),
        P(),
        P("col", None, None),
        P(("row", "col"), None),
        P(("row", "col")),
    )
    return jax.shard_map(
        on_device, mesh=mesh, in_specs=placed, out_specs=P(("row", "col"), None), check_vma=False
    )
```

```python
import functools

import jax
import jax.numpy as jnp
from jax import lax
from jax.experimental import pallas as pl
from jax.experimental.pallas import tpu as pltpu
from jax.sharding import PartitionSpec as P

MB = 8
LANES = 128
DEPTH = 2
PLACES = 16
BATCH = 4
MESH = pl.DeviceIdType.MESH
ANY = pl.BlockSpec(memory_space=pl.ANY)
VMEM = pl.BlockSpec(memory_space=pltpu.VMEM)
SMEM = pl.BlockSpec(memory_space=pltpu.SMEM)


def spread_kernel(axis, count, *refs):
    sources, targets = refs[:count], refs[count : 2 * count]
    sends, recvs, local = refs[2 * count :]
    me = lax.axis_index(axis)
    others = range(1, lax.axis_size(axis))

    def device(b):
        return {axis: lax.bitwise_xor(me, b)}

    barrier = pltpu.get_barrier_semaphore()
    for b in others:
        pl.semaphore_signal(barrier, inc=1, device_id=device(b), device_id_type=MESH)
    own = [
        pltpu.make_async_copy(source, target.at[me], local.at[k])
        for k, (source, target) in enumerate(zip(sources, targets))
    ]
    for copy in own:
        copy.start()
    pl.semaphore_wait(barrier, len(others))
    copies = []
    for k, (source, target) in enumerate(zip(sources, targets)):
        for b in others:
            copies.append(pltpu.make_async_remote_copy(
                source, target.at[me], sends.at[k, b], recvs.at[k, b],
                device_id=device(b), device_id_type=MESH))
            copies[-1].start()
    for copy in own + copies:
        copy.wait()


def spread(axis, size, number, arrays):
    count = len(arrays)
    return pl.pallas_call(
        functools.partial(spread_kernel, axis, count),
        out_shape=tuple(jax.ShapeDtypeStruct((size,) + a.shape, a.dtype) for a in arrays),
        in_specs=[VMEM] * count,
        out_specs=(VMEM,) * count,
        scratch_shapes=[
            pltpu.SemaphoreType.DMA((count, size)),
            pltpu.SemaphoreType.DMA((count, size)),
            pltpu.SemaphoreType.DMA((count,)),
        ],
        compiler_params=pltpu.CompilerParams(collective_id=number, has_side_effects=True),
        name="spread_" + axis,
    )(*arrays)


def apply_kernel(cols, depth, slot_ref, pick_ref, metric_ref, block_ref, *refs):
    outs, chosen, turned = refs[:cols], refs[cols], refs[cols + 1]
    lines = block_ref.shape[2] // LANES
    here = block_ref.shape[0]

    @pl.when(pl.program_id(0) == 0)
    def _():
        for e in range(chosen.shape[0]):
            chosen[e] = lax.dot_general(
                pick_ref[...], metric_ref[slot_ref[e]], (((1,), (1,)), ((), ())),
                preferred_element_type=jnp.float32).astype(jnp.bfloat16)

    for k in range(here):
        made = jnp.dot(
            chosen[pl.program_id(0) * here + k], block_ref[k], preferred_element_type=jnp.float32)
        total = made.shape[0]
        for start in range(0, total, 8):
            size = min(8, total - start)
            for line in range(lines):
                turned[k, pl.ds(start * lines + line, size, stride=lines), :] = made[
                    start : start + size, line * LANES : (line + 1) * LANES]
        for d in range(cols):
            for i in range(depth):
                row = (d * depth + i) * lines
                outs[d][i, k] = turned[k, row : row + lines, :].astype(jnp.bfloat16)


def apply_metric(cols, slot_ids, pick, metrics, integrals):
    listed, block_size, flat = integrals.shape
    lines = flat // LANES
    depth = pick.shape[0] // cols
    here = 3 if listed % 3 == 0 else 1
    shape = jax.ShapeDtypeStruct((depth, listed, lines, LANES), jnp.bfloat16)
    return pl.pallas_call(
        functools.partial(apply_kernel, cols, depth),
        grid=(listed // here,),
        out_shape=(shape,) * cols,
        in_specs=[SMEM, VMEM, VMEM, pl.BlockSpec((here, block_size, flat), lambda e: (e, 0, 0))],
        out_specs=(pl.BlockSpec((depth, here, lines, LANES), lambda e: (0, e, 0, 0)),) * cols,
        scratch_shapes=[
            pltpu.VMEM((listed, cols * depth, block_size), jnp.bfloat16),
            pltpu.VMEM((here, cols * depth * lines, LANES), jnp.float32),
        ],
        cost_estimate=pl.CostEstimate(flops=10**9, bytes_accessed=8 * 2**20, transcendentals=0),
        name="apply_metric",
    )(slot_ids, pick, metrics, integrals)


def build_kernel(cols, sizes, first, scale, corner_ref, second_ref, panel_ref, tile_ref, *refs):
    chunks, out_ref, acc = refs[:cols], refs[cols], refs[cols + 1]
    slots, side, block_size = sizes
    depth, listed, lines, _ = chunks[0].shape
    parity = LANES // block_size
    step = 6 if listed % 6 == 0 else 1
    acc[...] = jnp.zeros_like(acc)
    for d in range(cols):
        def entries(at, carry, d=d):
            made = []
            for k in range(step):
                e = at * step + k
                rows = chunks[d][:, pl.ds(e, 1)].reshape(depth * lines, LANES)
                made.append(jnp.dot(
                    rows, panel_ref[second_ref[d * listed + e]], preferred_element_type=jnp.float32))
            for k in range(step):
                corner = corner_ref[d * listed + at * step + k]
                for i in range(depth):
                    for odd in range(parity):
                        where = pl.ds(corner + odd, lines, stride=parity)
                        acc[i, where, :] += made[k][
                            i * lines : (i + 1) * lines, odd * LANES : (odd + 1) * LANES]
            return carry

        lax.fori_loop(0, listed // step, entries, 0)

    half = side // 2
    corners = ((0, 0), (0, 1), (1, 1))
    for a, b in corners:
        at = (slice(a * half, (a + 1) * half), slice(b * half, (b + 1) * half))
        out_ref[at] = jnp.zeros((half, half), jnp.float32) if first else tile_ref[at]
    batch = 4

    def products(group, carry):
        wide = jnp.concatenate(
            [
                acc[i, pl.ds(pl.multiple_of((group * batch + k) * side, side), side), :].astype(jnp.bfloat16)
                for k in range(batch)
                for i in range(depth)
            ],
            axis=1,
        )
        for a, b in corners:
            at = (slice(a * half, (a + 1) * half), slice(b * half, (b + 1) * half))
            out_ref[at] += lax.dot_general(
                wide[a * half : (a + 1) * half], wide[b * half : (b + 1) * half],
                (((1,), (1,)), ((), ())), preferred_element_type=jnp.float32)
        return carry

    lax.fori_loop(0, slots // batch, products, 0)
    if scale is not None:
        for a, b in corners:
            at = (slice(a * half, (a + 1) * half), slice(b * half, (b + 1) * half))
            out_ref[at] = out_ref[at] * scale
        out_ref[half:, :half] = out_ref[:half, half:].T


def build(cols, sizes, first, scale, corner, second, panels, tile, chunks):
    slots, side, _ = sizes
    depth = chunks[0].shape[0]
    return pl.pallas_call(
        functools.partial(build_kernel, cols, sizes, first, scale),
        out_shape=jax.ShapeDtypeStruct((side, side), jnp.float32),
        in_specs=[SMEM, SMEM, VMEM, VMEM] + [VMEM] * cols,
        out_specs=VMEM,
        scratch_shapes=[pltpu.VMEM((depth, slots * side, LANES), jnp.float32)],
        compiler_params=pltpu.CompilerParams(vmem_limit_bytes=56 * 2**20),
        cost_estimate=pl.CostEstimate(flops=10**10, bytes_accessed=8 * 2**20, transcendentals=0),
        name="build_tile",
    )(corner, second, panels, tile, *chunks)


def reduce_kernel(cols, tile_ref, out_ref, landed, crossing, crossed, sends, recvs):
    me_row, me_col = lax.axis_index("row"), lax.axis_index("col")
    share = out_ref.shape[0]
    half = cols // 2
    opposite = lax.bitwise_xor(me_col, half)

    def rows_of(col):
        return pl.ds(pl.multiple_of(col * share, share), share)

    barrier = pltpu.get_barrier_semaphore()
    for d in range(1, half + 1):
        pl.semaphore_signal(
            barrier, inc=1, device_id=(me_row, lax.bitwise_xor(me_col, d)), device_id_type=MESH)
    pl.semaphore_wait(barrier, half)
    near = []
    for side in (1, 0):
        for d in range(1, half):
            peer = lax.bitwise_xor(me_col, d)
            near.append(pltpu.make_async_remote_copy(
                tile_ref.at[rows_of(lax.bitwise_xor(peer, side * half))], landed.at[side, d - 1],
                sends.at[side, d - 1], recvs.at[side, d - 1], device_id=(me_row, peer), device_id_type=MESH))
            near[-1].start()
    total = tile_ref[rows_of(opposite), :]
    for d in range(1, half):
        near[d - 1].wait_recv()
        total = total + landed[1, d - 1]
    crossing[...] = total
    total = tile_ref[rows_of(me_col), :]
    out_ref[...] = total
    far = pltpu.make_async_remote_copy(
        crossing, crossed, sends.at[0, half - 1], recvs.at[0, half - 1],
        device_id=(me_row, opposite), device_id_type=MESH)
    far.start()
    for d in range(1, half):
        near[half - 2 + d].wait_recv()
        total = total + landed[0, d - 1]
    far.wait_recv()
    out_ref[...] = total + crossed[...]
    for copy in near:
        copy.wait_send()
    far.wait_send()


def reduce_tiles(cols, tile):
    side = tile.shape[0]
    half = cols // 2
    return pl.pallas_call(
        functools.partial(reduce_kernel, cols),
        out_shape=jax.ShapeDtypeStruct((side // cols, side), jnp.float32),
        in_specs=[VMEM],
        out_specs=VMEM,
        scratch_shapes=[
            pltpu.VMEM((2, half - 1, side // cols, side), jnp.float32),
            pltpu.VMEM((side // cols, side), jnp.float32),
            pltpu.VMEM((side // cols, side), jnp.float32),
            pltpu.SemaphoreType.DMA((2, half)),
            pltpu.SemaphoreType.DMA((2, half)),
        ],
        compiler_params=pltpu.CompilerParams(collective_id=1, has_side_effects=True),
        name="reduce_tiles",
    )(tile)


def in_phases(integrals, block_list, p_slot, metric, density_panel, pattern):
    rows, cols = lax.axis_size("row"), lax.axis_size("col")
    me_col = lax.axis_index("col")
    owned_slots, block_size = metric.shape[0], metric.shape[1]
    listed = integrals.shape[0]
    panel_width = density_panel.shape[1]
    slots = owned_slots * cols
    side = MB * block_size
    mine = block_size // cols
    depth = DEPTH if mine % DEPTH == 0 else 1
    phases = mine // depth
    metrics, panels_col, patterns_col, lists_col = spread(
        "col", cols, 0, (metric, density_panel, pattern.reshape(1, -1), block_list))
    metrics = metrics.reshape(slots, block_size, block_size)
    slot_match = block_list[:, 2][:, None] == jnp.arange(slots, dtype=jnp.int32)[None, :]
    slot_ids = jnp.sum(jnp.where(slot_match, p_slot[None, :], 0), axis=1)

    offsets = jnp.arange(cols, dtype=jnp.int32)
    peers = lax.bitwise_xor(offsets, me_col)
    places = jnp.arange(block_size, dtype=jnp.int32)
    sent = []
    for phase in range(phases):
        wanted = (peers[:, None] * mine + phase * depth + jnp.arange(depth, dtype=jnp.int32)).reshape(-1)
        pick = (wanted[:, None] == places[None, :]).astype(jnp.bfloat16)
        outgoing = apply_metric(cols, slot_ids, pick, metrics, integrals)
        arrived = [outgoing[0]]
        for d in range(1, cols):
            arrived.append(lax.ppermute(outgoing[d], "col", [(c, c ^ d) for c in range(cols)]))
        sent.append(arrived)
        if phase == 0:
            panels_col, patterns_col, lists_col, _ = lax.optimization_barrier(
                (panels_col, patterns_col, lists_col, outgoing[1]))

    panel_all, pattern_all = spread("row", rows, 2, (panels_col, patterns_col))
    panel_all = panel_all.reshape(-1, panel_width)
    panel_all = jnp.where(pattern_all.reshape(-1, 1) > 0, panel_all, jnp.zeros_like(panel_all))
    lists_in = jnp.sum(
        jnp.where((peers[:, None] == offsets[None, :])[:, :, None, None], lists_col[None], 0), axis=1)
    lists_in = lists_in.reshape(cols * listed, 3)
    match_in = lists_in[:, 2][:, None] == jnp.arange(slots, dtype=jnp.int32)[None, :]
    slots_in = jnp.sum(jnp.where(match_in, p_slot[None, :], 0), axis=1)
    corner = slots_in * side + (lists_in[:, 0] - lax.axis_index("row") * MB) * block_size
    second = lists_in[:, 1]
    parity = LANES // block_size
    blocks = panel_all.reshape(-1, block_size, panel_width)
    panels = jnp.concatenate(
        [
            jnp.pad(blocks, ((0, 0), (0, 0), (k * panel_width, (parity - 1 - k) * panel_width)))
            for k in range(parity)
        ],
        axis=1,
    )
    tile = jnp.zeros((8, LANES), jnp.float32)
    for phase in range(phases):
        last = phase == phases - 1
        scale = 1.0 / (slots * block_size * panel_width) if last else None
        tile = build(
            cols, (slots, side, block_size), phase == 0, scale, corner, second, panels, tile, sent[phase])
    return reduce_tiles(cols, tile)


def shapes_allow(rows, cols, listed, block_size, owned_slots, local_rows, panel_width, flat):
    slots = owned_slots * cols
    return (
        listed <= PLACES
        and listed % 4 == 0
        and cols * PLACES <= LANES
        and slots * MB <= LANES
        and slots % (BATCH * DEPTH) == 0
        and local_rows == block_size
        and rows * cols <= LANES
        and 2 * block_size == LANES
        and panel_width == LANES
        and flat == block_size * block_size
        and block_size % (cols * DEPTH) == 0
        and cols * DEPTH == 16
    )


def fused_kernel(rows, cols, cap, list_in, slot_in, pattern_in, density_in, metric_in, integrals_ref,
                 out_ref, flag_ref, list_ref, slot_ref, pattern_ref, density_ref, metric_ref, inputs, kept_rows, totals, lists, metrics, panels, blocks, made, pick, turned,
                 leaving, arriving, places, table, entry, packed, terms, halves, tile, landed, crossing, crossed,
                 loads, near_send, near_recv, row_send, row_recv, all_send, all_recv, sends, recvs, red_send,
                 red_recv, moved):
    f32, bf16, i32 = jnp.float32, jnp.bfloat16, jnp.int32
    me_row, me_col = lax.axis_index("row"), lax.axis_index("col")
    me = me_row * cols + me_col
    listed, block_size, flat = blocks.shape
    slots = metrics.shape[0]
    owned = slots // cols
    lines = flat // LANES
    phases = block_size // (cols * DEPTH)
    devices = rows * cols
    tiles = cap // LANES
    side = MB * block_size
    others = tuple(range(cols // 2, cols)) + tuple(range(1, cols // 2))
    everyone = [(r, c) for c in others + (0,) for r in range(rows) if r or c]

    def peer(r, c):
        return (lax.bitwise_xor(me_row, r), lax.bitwise_xor(me_col, c))

    barrier = pltpu.get_barrier_semaphore()
    for r, c in everyone:
        pl.semaphore_signal(barrier, inc=1, device_id=peer(r, c), device_id_type=MESH)
    own = pl.ds(me_col * owned, owned)
    small = [
        pltpu.make_async_copy(source, target, inputs.at[k])
        for k, (source, target) in enumerate((
            (pattern_in, pattern_ref),
            (list_in, list_ref),
            (slot_in, slot_ref),
            (metric_in, metric_ref),
            (density_in, density_ref),
        ))
    ]
    fetches = [pltpu.make_async_copy(integrals_ref.at[e], blocks.at[e], loads.at[e]) for e in range(listed)]
    for fetch in small + fetches:
        fetch.start()
    for fetch in small:
        fetch.wait()

    lane = lax.broadcasted_iota(i32, (1, LANES), 1)
    for e in range(PLACES):
        if e < listed:
            key = slot_ref[list_ref[2, e]] * MB + list_ref[0, e] - me_row * MB
            lists[me_col, e : e + 1, :] = jnp.where(lane < block_size, key, list_ref[1, e])
        else:
            lists[me_col, e : e + 1, :] = jnp.where(lane < block_size, 4 * LANES, 0)
    pattern = (pattern_ref[...] > 0).astype(i32)
    kept_rows[me] = jnp.concatenate([pattern, jnp.zeros_like(pattern)], axis=1)
    eye = lax.broadcasted_iota(i32, (block_size, block_size), 0) == lax.broadcasted_iota(
        i32, (block_size, block_size), 1)
    keep = jnp.sum(
        jnp.where(eye, jnp.broadcast_to(pattern.astype(f32), (block_size, block_size)), 0.0), axis=1, keepdims=True)
    panels[me] = jnp.where(keep > 0, density_ref[...].astype(f32), 0.0).astype(bf16)
    wanted = lax.broadcasted_iota(i32, (block_size, block_size), 0)
    wanted = (wanted // DEPTH % cols) * (block_size // cols) + wanted // (cols * DEPTH) * DEPTH + wanted % DEPTH
    order = (wanted == lax.broadcasted_iota(i32, (block_size, block_size), 1)).astype(bf16)
    for k in range(owned):
        metrics[me_col * owned + k] = lax.dot_general(
            order, metric_ref[k], (((1,), (1,)), ((), ())), preferred_element_type=f32).astype(bf16)

    pl.semaphore_wait(barrier, devices - 1)

    def share(ref, target, k, peers, send_sems, recv_sems):
        copies = [
            pltpu.make_async_remote_copy(
                ref, target, send_sems.at[k, r * cols + c], recv_sems.at[k, r * cols + c],
                device_id=peer(r, c), device_id_type=MESH)
            for r, c in peers
        ]
        for copy in copies:
            copy.start()
        return copies

    column = [(0, c) for c in others]
    kept_copies = share(kept_rows.at[me], kept_rows.at[me], 0, everyone, all_send, all_recv)
    metric_copies = share(metrics.at[own], metrics.at[own], 0, column, near_send, near_recv)
    list_copies = share(lists.at[me_col], lists.at[me_col], 1, column, near_send, near_recv)
    panel_copies = share(panels.at[me], panels.at[me], 2, column, near_send, near_recv)
    for copy in kept_copies:
        copy.wait_recv()

    square = (LANES, LANES)
    down, across = lax.broadcasted_iota(i32, square, 0), lax.broadcasted_iota(i32, square, 1)
    kept = kept_rows[:, 0, :].astype(f32)
    if devices < LANES:
        kept = jnp.concatenate([kept, jnp.zeros((LANES - devices, LANES), f32)], axis=0)
    running = jnp.dot(kept.astype(bf16), (down <= across).astype(bf16), preferred_element_type=f32)
    ranks = jnp.where(kept > 0, running - 1.0, -256.0).astype(bf16)

    def place(panel_of, count):
        row_id = lax.broadcasted_iota(i32, (count, LANES), 0)
        col_id = lax.broadcasted_iota(i32, (count, LANES), 1)
        real = (row_id % PLACES < listed) & (row_id < cols * PLACES)
        hot = ((panel_of == col_id) & real).astype(bf16)
        counts = jnp.sum(jnp.dot(hot, kept.astype(bf16), preferred_element_type=f32), axis=1, keepdims=True)
        before = lax.broadcasted_iota(i32, (count, count), 1)
        after = lax.broadcasted_iota(i32, (count, count), 0)
        ahead = ((after // PLACES == before // PLACES) & (before < after)).astype(bf16)
        starts = jnp.dot(
            ahead, jnp.broadcast_to(counts, (count, LANES)).astype(bf16), preferred_element_type=f32)
        rank = jnp.dot(hot, ranks, preferred_element_type=f32)
        spots = jnp.where(real & (rank >= 0) & (col_id < block_size), rank + starts, -1.0)
        return spots, jnp.sum(counts, axis=0, keepdims=True)

    spots, kept_here = place(lists[me_col, :, block_size : block_size + 1], PLACES)
    places[:PLACES, :] = spots
    totals[me] = jnp.broadcast_to(kept_here.astype(i32), (1, LANES))

    def choose(e, carry):
        spot = jnp.broadcast_to(places[pl.ds(e, 1), :], (block_size, LANES))
        half = lax.broadcasted_iota(i32, (block_size, LANES), 1)
        spot = jnp.sum(
            jnp.where(lax.broadcasted_iota(i32, (block_size, LANES), 0) == half, spot, 0.0), axis=1, keepdims=True)
        for t in range(tiles):
            pick[t, e] = (spot == (half + t * LANES).astype(f32)).astype(f32).astype(bf16)
        return carry

    lax.fori_loop(0, listed, choose, 0)

    for copy in metric_copies:
        copy.wait_recv()
    left_half = lax.broadcasted_iota(i32, (block_size, LANES), 1) < block_size

    def apply(pair, carry):
        factors = []
        for h in range(2):
            e = pair * 2 + h
            pltpu.make_async_copy(integrals_ref.at[e], blocks.at[e], loads.at[e]).wait()
            factors.append(metrics[slot_ref[list_ref[2, e]]])
        for j in range(lines // 2):
            both = [
                jnp.dot(
                    factors[h], blocks[pair * 2 + h, :, 2 * j * LANES : 2 * (j + 1) * LANES],
                    preferred_element_type=f32)
                for h in range(2)
            ]
            for half in range(2):
                a, b = (value[:, half * LANES : (half + 1) * LANES] for value in both)
                parts = (
                    jnp.where(left_half, a, pltpu.roll(b, block_size, 1)).astype(bf16),
                    jnp.where(left_half, pltpu.roll(a, block_size, 1), b).astype(bf16),
                )
                line = 2 * j + half
                for odd in range(2):
                    for p in range(phases):
                        made[p, pair, odd, line * 16 : (line + 1) * 16, :] = parts[odd][p * 16 : (p + 1) * 16, :]
        return carry

    lax.fori_loop(0, listed // 2, apply, 0)

    def passage(p, piece, k, d):
        c = lax.bitwise_xor(me_col, d)
        return pltpu.make_async_remote_copy(
            leaving.at[(p, c) + piece], arriving.at[(p, me_col) + piece], sends.at[p, k, d], recvs.at[p, k, d],
            device_id=(me_row, c), device_id_type=MESH)

    def by_parity(p, odd, d):
        return passage(p, (odd,), odd, d)

    def by_depth(p, i, d):
        return passage(p, (slice(None), i), i, d)

    def whole(p, d):
        return passage(p, (), 0, d)

    group = pl.ds(me_row * cols, cols)
    row_copies = [
        pltpu.make_async_remote_copy(
            panels.at[group], panels.at[group], row_send.at[r], row_recv.at[r],
            device_id=peer(r, 0), device_id_type=MESH)
        for r in range(rows - 1, 0, -1)
    ]

    def pack(p, carry):
        @pl.when(p == 1)
        def _():
            for copy in panel_copies:
                copy.wait_recv()
            for copy in row_copies:
                copy.start()

        def columns(odd, inner):
            left = jnp.concatenate([made[p, pair, odd] for pair in range(listed // 2)], axis=1)
            for t in range(0, tiles, 2):
                width = min(2, tiles - t)
                right = jnp.concatenate(
                    [pick[t + k].reshape(listed * block_size, LANES) for k in range(width)], axis=1)
                value = jnp.dot(left, right, preferred_element_type=f32)
                for line in range(lines):
                    for g in range(2):
                        for k in range(width):
                            turned[t + k, pl.ds(g * 8 * lines + line, 8, stride=lines), :] = value[
                                line * 16 + g * 8 : line * 16 + g * 8 + 8, k * LANES : (k + 1) * LANES]
            for c in range(cols):
                for i in range(DEPTH):
                    row = (c * DEPTH + i) * lines
                    leaving[p, c, odd, i] = turned[:, row : row + lines, :].astype(bf16)

            @pl.when(p == 0)
            def _():
                for d in others:
                    by_parity(p, odd, d).start()

            return inner

        lax.fori_loop(0, 2, columns, 0)

        @pl.when((p > 0) & (p < phases - 1))
        def _():
            for d in others:
                whole(p, d).start()

        @pl.when(p == phases - 1)
        def _():
            for i in range(DEPTH):
                for d in others:
                    by_depth(p, i, d).start()

        arriving[p, me_col] = leaving[p, me_col]
        return carry

    lax.fori_loop(0, phases, pack, 0)
    total_copies = share(totals.at[me], totals.at[me], 1, everyone, all_send, all_recv)
    for copy in list_copies:
        copy.wait_recv()
    mine = lists[...].reshape(cols * PLACES, LANES)
    if cols * PLACES < LANES:
        mine = jnp.concatenate([mine, jnp.full((LANES - cols * PLACES, LANES), 4 * LANES, i32)], axis=0)
    key = mine[:, 0:1]
    panel_of = mine[:, block_size : block_size + 1]
    places[...] = place(panel_of, LANES)[0]

    key_down = jnp.broadcast_to(key, square)
    key_across = jnp.broadcast_to(
        jnp.sum(jnp.where(down == across, key_down, 0), axis=0, keepdims=True), square)
    same_before = jnp.where((key_down == key_across) & (across < down), 1, 0)
    before = jnp.where(key_across < key_down, 1, 0) + same_before
    position = jnp.sum(before, axis=1, keepdims=True)
    repeats = jnp.minimum(jnp.sum(same_before, axis=1, keepdims=True), 1)
    at = position == across
    compact = down // PLACES * listed + down % PLACES
    table[0:1, :] = jnp.sum(jnp.where(at, compact, 0), axis=0, keepdims=True)
    table[1:2, :] = jnp.sum(jnp.where(at, repeats, 0), axis=0, keepdims=True)
    upto = jnp.sum(jnp.where(key_down <= across, 1, 0), axis=0, keepdims=True) - 1
    present = jnp.sum(jnp.where(key_down == across, 1, 0), axis=0, keepdims=True)
    table[2:3, :] = jnp.where(present > 0, upto, cols * listed)
    table[3:4, :] = jnp.sum(jnp.where(down == across, panel_of, 0), axis=0, keepdims=True)
    table[4:8, :] = jnp.zeros((4, LANES), i32)
    down_table = pltpu.make_async_copy(table, entry, moved)
    down_table.start()

    halves[cols * listed] = jnp.zeros((DEPTH, block_size, LANES), bf16)
    for a in range(2):
        tile[a * (side // 2) : (a + 1) * (side // 2), :] = jnp.zeros((side // 2, side), f32)
    down_table.wait()
    for copy in row_copies:
        copy.wait_recv()

    def gather(at_pair, carry):
        c, pair = at_pair // (listed // 2), at_pair % (listed // 2)
        for h in range(2):
            place = c * PLACES + pair * 2 + h
            spot = jnp.broadcast_to(places[pl.ds(place, 1), :][:, :block_size], (cap, block_size))
            chosen_rows = (spot == lax.broadcasted_iota(i32, (cap, block_size), 0).astype(f32)).astype(f32).astype(bf16)
            packed[c, pair, :, h * LANES : (h + 1) * LANES] = jnp.dot(
                chosen_rows, panels[entry[3, place]], preferred_element_type=f32).astype(bf16)
        return carry

    lax.fori_loop(0, cols * (listed // 2), gather, 0)

    def phase(p, first, count, arrived):
        def source(d, inner):
            c = lax.bitwise_xor(me_col, d)

            @pl.when(d > 0)
            def _():
                arrived(p, d)

            left = jnp.concatenate(
                [
                    jnp.concatenate([arriving[p, c, odd, first + i, t] for t in range(tiles)], axis=1)
                    for odd in range(2)
                    for i in range(count)
                ],
                axis=0,
            )
            for pair in range(listed // 2):
                value = jnp.dot(left, packed[c, pair], preferred_element_type=f32)
                for h in range(2):
                    for odd in range(2):
                        for i in range(count):
                            row = (odd * count + i) * lines
                            terms[c * listed + pair * 2 + h, i, pl.ds(odd, lines, stride=2), :] = value[
                                row : row + lines, h * LANES : (h + 1) * LANES]
            return inner

        lax.fori_loop(0, cols, source, 0)

        def segment(r, total):
            for k in range(4):
                at = r * 4 + k
                again = entry[1, at].astype(f32)
                total = terms[entry[0, at]][:count] + total * again
                halves[at, :count] = total.astype(bf16)
            return total

        lax.fori_loop(0, cols * listed // 4, segment, jnp.zeros((count, block_size, LANES), f32))

        batch = BATCH * DEPTH // count

        def products(s, inner):
            strip = []
            for a in range(MB):
                parts = []
                for k in range(batch):
                    cell = halves[entry[2, (s * batch + k) * MB + a]]
                    parts.extend(cell[i] for i in range(count))
                strip.append(jnp.concatenate(parts, axis=1))
            high = jnp.concatenate(strip[: MB // 2], axis=0)
            low = jnp.concatenate(strip[MB // 2 :], axis=0)
            half = side // 2
            for left, right, a, b in ((high, high, 0, 0), (high, low, 0, 1), (low, low, 1, 1)):
                tile[a * half : (a + 1) * half, b * half : (b + 1) * half] += lax.dot_general(
                    left, right, (((1,), (1,)), ((), ())), preferred_element_type=f32)
            return inner

        lax.fori_loop(0, slots // batch, products, 0)

    def early(p, carry):
        def arrived(p, d):
            @pl.when(p == 0)
            def _():
                for odd in range(2):
                    by_parity(p, odd, d).wait_recv()

            @pl.when(p > 0)
            def _():
                whole(p, d).wait_recv()

        phase(p, 0, DEPTH, arrived)
        return carry

    lax.fori_loop(0, phases - 1, early, 0)

    def late(i, carry):
        phase(phases - 1, i, 1, lambda p, d: by_depth(p, i, d).wait_recv())
        return carry

    lax.fori_loop(0, DEPTH, late, 0)
    half = side // 2
    tile[half:, :half] = tile[:half, half:].T

    scale = 1.0 / (slots * block_size * LANES)
    share = out_ref.shape[0]
    middle = cols // 2
    opposite = lax.bitwise_xor(me_col, middle)

    def rows_of(col):
        return pl.ds(pl.multiple_of(col * share, share), share)

    strips = [pl.ds(q * (side // 2), side // 2) for q in range(2)]
    near = {}
    for far_side, q in ((1, 0), (1, 1), (0, 0), (0, 1)):
        for d in range(1, middle):
            target = lax.bitwise_xor(me_col, d)
            near[far_side, q, d] = pltpu.make_async_remote_copy(
                tile.at[rows_of(lax.bitwise_xor(target, far_side * middle)), strips[q]],
                landed.at[far_side, d - 1, :, strips[q]],
                red_send.at[far_side, q, d], red_recv.at[far_side, q, d],
                device_id=(me_row, target), device_id_type=MESH)
            near[far_side, q, d].start()
    far = []
    for q in range(2):
        total = tile[rows_of(opposite), strips[q]]
        for d in range(1, middle):
            near[1, q, d].wait_recv()
            total = total + landed[1, d - 1, :, strips[q]]
        crossing[q] = total
        far.append(pltpu.make_async_remote_copy(
            crossing.at[q], crossed.at[q], red_send.at[0, q, 0], red_recv.at[0, q, 0],
            device_id=(me_row, opposite), device_id_type=MESH))
        far[-1].start()
    for copy in total_copies:
        copy.wait_recv()
    table[0:1, :] = jnp.max(totals[:, 0, :], axis=0, keepdims=True)
    verdict = pltpu.make_async_copy(table, entry, moved)
    verdict.start()
    for q in range(2):
        total = tile[rows_of(me_col), strips[q]]
        for d in range(1, middle):
            near[0, q, d].wait_recv()
            total = total + landed[0, d - 1, :, strips[q]]
        far[q].wait_recv()
        out_ref[:, strips[q]] = (total + crossed[q]) * scale
    verdict.wait()
    flag_ref[0] = (entry[0, 0] <= cap).astype(i32)
    copies = metric_copies + kept_copies + list_copies + panel_copies + row_copies + total_copies
    for copy in copies + list(near.values()) + far:
        copy.wait_send()

    def finish(p, carry):
        for d in others:
            whole(p, d).wait_send()
        return carry

    lax.fori_loop(1, phases - 1, finish, 0)
    for d in others:
        for k in range(2):
            by_parity(0, k, d).wait_send()
            by_depth(phases - 1, k, d).wait_send()


def fused(integrals, block_list, p_slot, metric, density_panel, pattern):
    rows, cols = lax.axis_size("row"), lax.axis_size("col")
    listed, block_size, flat = integrals.shape
    slots = metric.shape[0] * cols
    devices = rows * cols
    side = MB * block_size
    lines = flat // LANES
    phases = block_size // (cols * DEPTH)
    cap = -(-(listed * block_size * 5 // 6) // LANES) * LANES
    tiles = cap // LANES
    bf16, f32, i32 = jnp.bfloat16, jnp.float32, jnp.int32
    half = cols // 2
    dma = pltpu.SemaphoreType.DMA
    out, flag = pl.pallas_call(
        functools.partial(fused_kernel, rows, cols, cap),
        out_shape=(
            jax.ShapeDtypeStruct((side // cols, side), f32),
            jax.ShapeDtypeStruct((1,), i32),
        ),
        in_specs=[ANY] * 6,
        out_specs=(VMEM, SMEM),
        scratch_shapes=[
            pltpu.SMEM((3, listed), i32),
            pltpu.SMEM(p_slot.shape, i32),
            pltpu.VMEM((1, block_size), i32),
            pltpu.VMEM(density_panel.shape, bf16),
            pltpu.VMEM(metric.shape, bf16),
            dma((5,)),
            pltpu.VMEM((devices, 1, LANES), i32),
            pltpu.VMEM((devices, 1, LANES), i32),
            pltpu.VMEM((cols, PLACES, LANES), i32),
            pltpu.VMEM((slots, block_size, block_size), bf16),
            pltpu.VMEM((devices, block_size, LANES), bf16),
            pltpu.VMEM((listed, block_size, flat), bf16),
            pltpu.VMEM((phases, listed // 2, 2, lines * 16, LANES), bf16),
            pltpu.VMEM((tiles, listed, block_size, LANES), bf16),
            pltpu.VMEM((tiles, 16 * lines, LANES), f32),
            pltpu.VMEM((phases, cols, 2, DEPTH, tiles, lines, LANES), bf16),
            pltpu.VMEM((phases, cols, 2, DEPTH, tiles, lines, LANES), bf16),
            pltpu.VMEM((LANES, LANES), f32),
            pltpu.VMEM((8, LANES), i32),
            pltpu.SMEM((8, LANES), i32),
            pltpu.VMEM((cols, listed // 2, cap, 2 * LANES), bf16),
            pltpu.VMEM((cols * listed, DEPTH, block_size, LANES), f32),
            pltpu.VMEM((cols * listed + 1, DEPTH, block_size, LANES), bf16),
            pltpu.VMEM((side, side), f32),
            pltpu.VMEM((2, half - 1, side // cols, side), f32),
            pltpu.VMEM((2, side // cols, side // 2), f32),
            pltpu.VMEM((2, side // cols, side // 2), f32),
            dma((listed,)),
            dma((3, cols)),
            dma((3, cols)),
            dma((rows,)),
            dma((rows,)),
            dma((2, devices)),
            dma((2, devices)),
            dma((phases, 2, cols)),
            dma((phases, 2, cols)),
            dma((2, 2, half)),
            dma((2, 2, half)),
            dma,
        ],
        compiler_params=pltpu.CompilerParams(
            collective_id=3, has_side_effects=True, vmem_limit_bytes=63 * 2**20),
        name="fused",
    )(block_list.T, p_slot, pattern.reshape(1, -1), density_panel, metric, integrals)
    return out, flag


def on_device(integrals, block_list, p_slot, metric, density_panel, pattern):
    arguments = (integrals, block_list, p_slot, metric, density_panel, pattern)
    listed, block_size, flat = integrals.shape
    if not shapes_allow(
        lax.axis_size("row"), lax.axis_size("col"), listed, block_size, metric.shape[0],
        density_panel.shape[0], density_panel.shape[1], flat,
    ):
        return in_phases(*arguments)
    out, flag = fused(*arguments)
    return lax.cond(flag[0] > 0, lambda *_: out, in_phases, *arguments)


def solution(mesh):
    placed = (
        P(("row", "col"), None, None),
        P(("row", "col"), None),
        P(),
        P("col", None, None),
        P(("row", "col"), None),
        P(("row", "col")),
    )
    return jax.shard_map(
        on_device, mesh=mesh, in_specs=placed, out_specs=P(("row", "col"), None), check_vma=False
    )
```

```python
import functools

import jax
import jax.numpy as jnp
from jax import lax
from jax.experimental import pallas as pl
from jax.experimental.pallas import tpu as pltpu
from jax.sharding import PartitionSpec as P

MB = 8
LANES = 128
DEPTH = 2
PLACES = 16
BATCH = 4
MESH = pl.DeviceIdType.MESH
ANY = pl.BlockSpec(memory_space=pl.ANY)
VMEM = pl.BlockSpec(memory_space=pltpu.VMEM)
SMEM = pl.BlockSpec(memory_space=pltpu.SMEM)


def spread_kernel(axis, count, *refs):
    sources, targets = refs[:count], refs[count : 2 * count]
    sends, recvs, local = refs[2 * count :]
    me = lax.axis_index(axis)
    others = range(1, lax.axis_size(axis))

    def device(b):
        return {axis: lax.bitwise_xor(me, b)}

    barrier = pltpu.get_barrier_semaphore()
    for b in others:
        pl.semaphore_signal(barrier, inc=1, device_id=device(b), device_id_type=MESH)
    own = [
        pltpu.make_async_copy(source, target.at[me], local.at[k])
        for k, (source, target) in enumerate(zip(sources, targets))
    ]
    for copy in own:
        copy.start()
    pl.semaphore_wait(barrier, len(others))
    copies = []
    for k, (source, target) in enumerate(zip(sources, targets)):
        for b in others:
            copies.append(pltpu.make_async_remote_copy(
                source, target.at[me], sends.at[k, b], recvs.at[k, b],
                device_id=device(b), device_id_type=MESH))
            copies[-1].start()
    for copy in own + copies:
        copy.wait()


def spread(axis, size, number, arrays):
    count = len(arrays)
    return pl.pallas_call(
        functools.partial(spread_kernel, axis, count),
        out_shape=tuple(jax.ShapeDtypeStruct((size,) + a.shape, a.dtype) for a in arrays),
        in_specs=[VMEM] * count,
        out_specs=(VMEM,) * count,
        scratch_shapes=[
            pltpu.SemaphoreType.DMA((count, size)),
            pltpu.SemaphoreType.DMA((count, size)),
            pltpu.SemaphoreType.DMA((count,)),
        ],
        compiler_params=pltpu.CompilerParams(collective_id=number, has_side_effects=True),
        name="spread_" + axis,
    )(*arrays)


def apply_kernel(cols, depth, slot_ref, pick_ref, metric_ref, block_ref, *refs):
    outs, chosen, turned = refs[:cols], refs[cols], refs[cols + 1]
    lines = block_ref.shape[2] // LANES
    here = block_ref.shape[0]

    @pl.when(pl.program_id(0) == 0)
    def _():
        for e in range(chosen.shape[0]):
            chosen[e] = lax.dot_general(
                pick_ref[...], metric_ref[slot_ref[e]], (((1,), (1,)), ((), ())),
                preferred_element_type=jnp.float32).astype(jnp.bfloat16)

    for k in range(here):
        made = jnp.dot(
            chosen[pl.program_id(0) * here + k], block_ref[k], preferred_element_type=jnp.float32)
        total = made.shape[0]
        for start in range(0, total, 8):
            size = min(8, total - start)
            for line in range(lines):
                turned[k, pl.ds(start * lines + line, size, stride=lines), :] = made[
                    start : start + size, line * LANES : (line + 1) * LANES]
        for d in range(cols):
            for i in range(depth):
                row = (d * depth + i) * lines
                outs[d][i, k] = turned[k, row : row + lines, :].astype(jnp.bfloat16)


def apply_metric(cols, slot_ids, pick, metrics, integrals):
    listed, block_size, flat = integrals.shape
    lines = flat // LANES
    depth = pick.shape[0] // cols
    here = 3 if listed % 3 == 0 else 1
    shape = jax.ShapeDtypeStruct((depth, listed, lines, LANES), jnp.bfloat16)
    return pl.pallas_call(
        functools.partial(apply_kernel, cols, depth),
        grid=(listed // here,),
        out_shape=(shape,) * cols,
        in_specs=[SMEM, VMEM, VMEM, pl.BlockSpec((here, block_size, flat), lambda e: (e, 0, 0))],
        out_specs=(pl.BlockSpec((depth, here, lines, LANES), lambda e: (0, e, 0, 0)),) * cols,
        scratch_shapes=[
            pltpu.VMEM((listed, cols * depth, block_size), jnp.bfloat16),
            pltpu.VMEM((here, cols * depth * lines, LANES), jnp.float32),
        ],
        cost_estimate=pl.CostEstimate(flops=10**9, bytes_accessed=8 * 2**20, transcendentals=0),
        name="apply_metric",
    )(slot_ids, pick, metrics, integrals)


def build_kernel(cols, sizes, first, scale, corner_ref, second_ref, panel_ref, tile_ref, *refs):
    chunks, out_ref, acc = refs[:cols], refs[cols], refs[cols + 1]
    slots, side, block_size = sizes
    depth, listed, lines, _ = chunks[0].shape
    parity = LANES // block_size
    step = 6 if listed % 6 == 0 else 1
    acc[...] = jnp.zeros_like(acc)
    for d in range(cols):
        def entries(at, carry, d=d):
            made = []
            for k in range(step):
                e = at * step + k
                rows = chunks[d][:, pl.ds(e, 1)].reshape(depth * lines, LANES)
                made.append(jnp.dot(
                    rows, panel_ref[second_ref[d * listed + e]], preferred_element_type=jnp.float32))
            for k in range(step):
                corner = corner_ref[d * listed + at * step + k]
                for i in range(depth):
                    for odd in range(parity):
                        where = pl.ds(corner + odd, lines, stride=parity)
                        acc[i, where, :] += made[k][
                            i * lines : (i + 1) * lines, odd * LANES : (odd + 1) * LANES]
            return carry

        lax.fori_loop(0, listed // step, entries, 0)

    half = side // 2
    corners = ((0, 0), (0, 1), (1, 1))
    for a, b in corners:
        at = (slice(a * half, (a + 1) * half), slice(b * half, (b + 1) * half))
        out_ref[at] = jnp.zeros((half, half), jnp.float32) if first else tile_ref[at]
    batch = 4

    def products(group, carry):
        wide = jnp.concatenate(
            [
                acc[i, pl.ds(pl.multiple_of((group * batch + k) * side, side), side), :].astype(jnp.bfloat16)
                for k in range(batch)
                for i in range(depth)
            ],
            axis=1,
        )
        for a, b in corners:
            at = (slice(a * half, (a + 1) * half), slice(b * half, (b + 1) * half))
            out_ref[at] += lax.dot_general(
                wide[a * half : (a + 1) * half], wide[b * half : (b + 1) * half],
                (((1,), (1,)), ((), ())), preferred_element_type=jnp.float32)
        return carry

    lax.fori_loop(0, slots // batch, products, 0)
    if scale is not None:
        for a, b in corners:
            at = (slice(a * half, (a + 1) * half), slice(b * half, (b + 1) * half))
            out_ref[at] = out_ref[at] * scale
        out_ref[half:, :half] = out_ref[:half, half:].T


def build(cols, sizes, first, scale, corner, second, panels, tile, chunks):
    slots, side, _ = sizes
    depth = chunks[0].shape[0]
    return pl.pallas_call(
        functools.partial(build_kernel, cols, sizes, first, scale),
        out_shape=jax.ShapeDtypeStruct((side, side), jnp.float32),
        in_specs=[SMEM, SMEM, VMEM, VMEM] + [VMEM] * cols,
        out_specs=VMEM,
        scratch_shapes=[pltpu.VMEM((depth, slots * side, LANES), jnp.float32)],
        compiler_params=pltpu.CompilerParams(vmem_limit_bytes=56 * 2**20),
        cost_estimate=pl.CostEstimate(flops=10**10, bytes_accessed=8 * 2**20, transcendentals=0),
        name="build_tile",
    )(corner, second, panels, tile, *chunks)


def reduce_kernel(cols, tile_ref, out_ref, landed, crossing, crossed, sends, recvs):
    me_row, me_col = lax.axis_index("row"), lax.axis_index("col")
    share = out_ref.shape[0]
    half = cols // 2
    opposite = lax.bitwise_xor(me_col, half)

    def rows_of(col):
        return pl.ds(pl.multiple_of(col * share, share), share)

    barrier = pltpu.get_barrier_semaphore()
    for d in range(1, half + 1):
        pl.semaphore_signal(
            barrier, inc=1, device_id=(me_row, lax.bitwise_xor(me_col, d)), device_id_type=MESH)
    pl.semaphore_wait(barrier, half)
    near = []
    for side in (1, 0):
        for d in range(1, half):
            peer = lax.bitwise_xor(me_col, d)
            near.append(pltpu.make_async_remote_copy(
                tile_ref.at[rows_of(lax.bitwise_xor(peer, side * half))], landed.at[side, d - 1],
                sends.at[side, d - 1], recvs.at[side, d - 1], device_id=(me_row, peer), device_id_type=MESH))
            near[-1].start()
    total = tile_ref[rows_of(opposite), :]
    for d in range(1, half):
        near[d - 1].wait_recv()
        total = total + landed[1, d - 1]
    crossing[...] = total
    total = tile_ref[rows_of(me_col), :]
    out_ref[...] = total
    far = pltpu.make_async_remote_copy(
        crossing, crossed, sends.at[0, half - 1], recvs.at[0, half - 1],
        device_id=(me_row, opposite), device_id_type=MESH)
    far.start()
    for d in range(1, half):
        near[half - 2 + d].wait_recv()
        total = total + landed[0, d - 1]
    far.wait_recv()
    out_ref[...] = total + crossed[...]
    for copy in near:
        copy.wait_send()
    far.wait_send()


def reduce_tiles(cols, tile):
    side = tile.shape[0]
    half = cols // 2
    return pl.pallas_call(
        functools.partial(reduce_kernel, cols),
        out_shape=jax.ShapeDtypeStruct((side // cols, side), jnp.float32),
        in_specs=[VMEM],
        out_specs=VMEM,
        scratch_shapes=[
            pltpu.VMEM((2, half - 1, side // cols, side), jnp.float32),
            pltpu.VMEM((side // cols, side), jnp.float32),
            pltpu.VMEM((side // cols, side), jnp.float32),
            pltpu.SemaphoreType.DMA((2, half)),
            pltpu.SemaphoreType.DMA((2, half)),
        ],
        compiler_params=pltpu.CompilerParams(collective_id=1, has_side_effects=True),
        name="reduce_tiles",
    )(tile)


def in_phases(integrals, block_list, p_slot, metric, density_panel, pattern):
    rows, cols = lax.axis_size("row"), lax.axis_size("col")
    me_col = lax.axis_index("col")
    owned_slots, block_size = metric.shape[0], metric.shape[1]
    listed = integrals.shape[0]
    panel_width = density_panel.shape[1]
    slots = owned_slots * cols
    side = MB * block_size
    mine = block_size // cols
    depth = DEPTH if mine % DEPTH == 0 else 1
    phases = mine // depth
    metrics, panels_col, patterns_col, lists_col = spread(
        "col", cols, 0, (metric, density_panel, pattern.reshape(1, -1), block_list))
    metrics = metrics.reshape(slots, block_size, block_size)
    slot_match = block_list[:, 2][:, None] == jnp.arange(slots, dtype=jnp.int32)[None, :]
    slot_ids = jnp.sum(jnp.where(slot_match, p_slot[None, :], 0), axis=1)

    offsets = jnp.arange(cols, dtype=jnp.int32)
    peers = lax.bitwise_xor(offsets, me_col)
    places = jnp.arange(block_size, dtype=jnp.int32)
    sent = []
    for phase in range(phases):
        wanted = (peers[:, None] * mine + phase * depth + jnp.arange(depth, dtype=jnp.int32)).reshape(-1)
        pick = (wanted[:, None] == places[None, :]).astype(jnp.bfloat16)
        outgoing = apply_metric(cols, slot_ids, pick, metrics, integrals)
        arrived = [outgoing[0]]
        for d in range(1, cols):
            arrived.append(lax.ppermute(outgoing[d], "col", [(c, c ^ d) for c in range(cols)]))
        sent.append(arrived)
        if phase == 0:
            panels_col, patterns_col, lists_col, _ = lax.optimization_barrier(
                (panels_col, patterns_col, lists_col, outgoing[1]))

    panel_all, pattern_all = spread("row", rows, 2, (panels_col, patterns_col))
    panel_all = panel_all.reshape(-1, panel_width)
    panel_all = jnp.where(pattern_all.reshape(-1, 1) > 0, panel_all, jnp.zeros_like(panel_all))
    lists_in = jnp.sum(
        jnp.where((peers[:, None] == offsets[None, :])[:, :, None, None], lists_col[None], 0), axis=1)
    lists_in = lists_in.reshape(cols * listed, 3)
    match_in = lists_in[:, 2][:, None] == jnp.arange(slots, dtype=jnp.int32)[None, :]
    slots_in = jnp.sum(jnp.where(match_in, p_slot[None, :], 0), axis=1)
    corner = slots_in * side + (lists_in[:, 0] - lax.axis_index("row") * MB) * block_size
    second = lists_in[:, 1]
    parity = LANES // block_size
    blocks = panel_all.reshape(-1, block_size, panel_width)
    panels = jnp.concatenate(
        [
            jnp.pad(blocks, ((0, 0), (0, 0), (k * panel_width, (parity - 1 - k) * panel_width)))
            for k in range(parity)
        ],
        axis=1,
    )
    tile = jnp.zeros((8, LANES), jnp.float32)
    for phase in range(phases):
        last = phase == phases - 1
        scale = 1.0 / (slots * block_size * panel_width) if last else None
        tile = build(
            cols, (slots, side, block_size), phase == 0, scale, corner, second, panels, tile, sent[phase])
    return reduce_tiles(cols, tile)


def shapes_allow(rows, cols, listed, block_size, owned_slots, local_rows, panel_width, flat):
    slots = owned_slots * cols
    return (
        listed <= PLACES
        and listed % 4 == 0
        and cols * PLACES <= LANES
        and slots * MB <= LANES
        and slots % (BATCH * DEPTH) == 0
        and local_rows == block_size
        and rows * cols <= LANES
        and 2 * block_size == LANES
        and panel_width == LANES
        and flat == block_size * block_size
        and block_size % (cols * DEPTH) == 0
        and cols * DEPTH == 16
    )


def fused_kernel(rows, cols, cap, list_in, slot_in, pattern_in, density_in, metric_in, integrals_ref,
                 out_ref, flag_ref, list_ref, slot_ref, pattern_ref, density_ref, metric_ref, inputs, kept_rows, totals, lists, metrics, panels, blocks, made, pick, turned,
                 leaving, arriving, places, table, entry, packed, terms, halves, tile, landed, crossing, crossed,
                 loads, near_send, near_recv, row_send, row_recv, all_send, all_recv, sends, recvs, red_send,
                 red_recv, moved):
    f32, bf16, i32 = jnp.float32, jnp.bfloat16, jnp.int32
    me_row, me_col = lax.axis_index("row"), lax.axis_index("col")
    me = me_row * cols + me_col
    listed, block_size, flat = blocks.shape
    slots = metrics.shape[0]
    owned = slots // cols
    lines = flat // LANES
    phases = block_size // (cols * DEPTH)
    devices = rows * cols
    tiles = cap // LANES
    side = MB * block_size
    others = tuple(range(cols // 2, cols)) + tuple(range(1, cols // 2))
    everyone = [(r, c) for c in others + (0,) for r in range(rows) if r or c]

    def peer(r, c):
        return (lax.bitwise_xor(me_row, r), lax.bitwise_xor(me_col, c))

    barrier = pltpu.get_barrier_semaphore()
    for r, c in everyone:
        pl.semaphore_signal(barrier, inc=1, device_id=peer(r, c), device_id_type=MESH)
    own = pl.ds(me_col * owned, owned)
    small = [
        pltpu.make_async_copy(source, target, inputs.at[k])
        for k, (source, target) in enumerate((
            (pattern_in, pattern_ref),
            (list_in, list_ref),
            (slot_in, slot_ref),
            (metric_in, metric_ref),
            (density_in, density_ref),
        ))
    ]
    fetches = [pltpu.make_async_copy(integrals_ref.at[e], blocks.at[e], loads.at[e]) for e in range(listed)]
    for fetch in small + fetches:
        fetch.start()
    for fetch in small:
        fetch.wait()

    lane = lax.broadcasted_iota(i32, (1, LANES), 1)
    for e in range(PLACES):
        if e < listed:
            key = slot_ref[list_ref[2, e]] * MB + list_ref[0, e] - me_row * MB
            lists[me_col, e : e + 1, :] = jnp.where(lane < block_size, key, list_ref[1, e])
        else:
            lists[me_col, e : e + 1, :] = jnp.where(lane < block_size, 4 * LANES, 0)
    pattern = (pattern_ref[...] > 0).astype(i32)
    kept_rows[me] = jnp.concatenate([pattern, jnp.zeros_like(pattern)], axis=1)
    eye = lax.broadcasted_iota(i32, (block_size, block_size), 0) == lax.broadcasted_iota(
        i32, (block_size, block_size), 1)
    keep = jnp.sum(
        jnp.where(eye, jnp.broadcast_to(pattern.astype(f32), (block_size, block_size)), 0.0), axis=1, keepdims=True)
    panels[me] = jnp.where(keep > 0, density_ref[...].astype(f32), 0.0).astype(bf16)
    wanted = lax.broadcasted_iota(i32, (block_size, block_size), 0)
    wanted = (wanted // DEPTH % cols) * (block_size // cols) + wanted // (cols * DEPTH) * DEPTH + wanted % DEPTH
    order = (wanted == lax.broadcasted_iota(i32, (block_size, block_size), 1)).astype(bf16)
    for k in range(owned):
        metrics[me_col * owned + k] = lax.dot_general(
            order, metric_ref[k], (((1,), (1,)), ((), ())), preferred_element_type=f32).astype(bf16)

    pl.semaphore_wait(barrier, devices - 1)

    def share(ref, target, k, peers, send_sems, recv_sems):
        copies = [
            pltpu.make_async_remote_copy(
                ref, target, send_sems.at[k, r * cols + c], recv_sems.at[k, r * cols + c],
                device_id=peer(r, c), device_id_type=MESH)
            for r, c in peers
        ]
        for copy in copies:
            copy.start()
        return copies

    column = [(0, c) for c in others]
    kept_copies = share(kept_rows.at[me], kept_rows.at[me], 0, everyone, all_send, all_recv)
    metric_copies = share(metrics.at[own], metrics.at[own], 0, column, near_send, near_recv)
    list_copies = share(lists.at[me_col], lists.at[me_col], 1, column, near_send, near_recv)
    panel_copies = share(panels.at[me], panels.at[me], 2, column, near_send, near_recv)
    for copy in kept_copies:
        copy.wait_recv()

    square = (LANES, LANES)
    down, across = lax.broadcasted_iota(i32, square, 0), lax.broadcasted_iota(i32, square, 1)
    kept = kept_rows[:, 0, :].astype(f32)
    if devices < LANES:
        kept = jnp.concatenate([kept, jnp.zeros((LANES - devices, LANES), f32)], axis=0)
    running = jnp.dot(kept.astype(bf16), (down <= across).astype(bf16), preferred_element_type=f32)
    ranks = jnp.where(kept > 0, running - 1.0, -256.0).astype(bf16)

    def place(panel_of, count):
        row_id = lax.broadcasted_iota(i32, (count, LANES), 0)
        col_id = lax.broadcasted_iota(i32, (count, LANES), 1)
        real = (row_id % PLACES < listed) & (row_id < cols * PLACES)
        hot = ((panel_of == col_id) & real).astype(bf16)
        counts = jnp.sum(jnp.dot(hot, kept.astype(bf16), preferred_element_type=f32), axis=1, keepdims=True)
        before = lax.broadcasted_iota(i32, (count, count), 1)
        after = lax.broadcasted_iota(i32, (count, count), 0)
        ahead = ((after // PLACES == before // PLACES) & (before < after)).astype(bf16)
        starts = jnp.dot(
            ahead, jnp.broadcast_to(counts, (count, LANES)).astype(bf16), preferred_element_type=f32)
        rank = jnp.dot(hot, ranks, preferred_element_type=f32)
        spots = jnp.where(real & (rank >= 0) & (col_id < block_size), rank + starts, -1.0)
        return spots, jnp.sum(counts, axis=0, keepdims=True)

    spots, kept_here = place(lists[me_col, :, block_size : block_size + 1], PLACES)
    places[:PLACES, :] = spots
    totals[me] = jnp.broadcast_to(kept_here.astype(i32), (1, LANES))

    def choose(e, carry):
        spot = jnp.broadcast_to(places[pl.ds(e, 1), :], (block_size, LANES))
        half = lax.broadcasted_iota(i32, (block_size, LANES), 1)
        spot = jnp.sum(
            jnp.where(lax.broadcasted_iota(i32, (block_size, LANES), 0) == half, spot, 0.0), axis=1, keepdims=True)
        for t in range(tiles):
            pick[t, e] = (spot == (half + t * LANES).astype(f32)).astype(f32).astype(bf16)
        return carry

    lax.fori_loop(0, listed, choose, 0)

    for copy in metric_copies:
        copy.wait_recv()
    left_half = lax.broadcasted_iota(i32, (block_size, LANES), 1) < block_size

    def apply(pair, carry):
        factors = []
        for h in range(2):
            e = pair * 2 + h
            pltpu.make_async_copy(integrals_ref.at[e], blocks.at[e], loads.at[e]).wait()
            factors.append(metrics[slot_ref[list_ref[2, e]]])
        for j in range(lines // 2):
            both = [
                jnp.dot(
                    factors[h], blocks[pair * 2 + h, :, 2 * j * LANES : 2 * (j + 1) * LANES],
                    preferred_element_type=f32)
                for h in range(2)
            ]
            for half in range(2):
                a, b = (value[:, half * LANES : (half + 1) * LANES] for value in both)
                parts = (
                    jnp.where(left_half, a, pltpu.roll(b, block_size, 1)).astype(bf16),
                    jnp.where(left_half, pltpu.roll(a, block_size, 1), b).astype(bf16),
                )
                line = 2 * j + half
                for odd in range(2):
                    for p in range(phases):
                        made[p, pair, odd, line * 16 : (line + 1) * 16, :] = parts[odd][p * 16 : (p + 1) * 16, :]
        return carry

    lax.fori_loop(0, listed // 2, apply, 0)

    def passage(p, piece, k, d):
        c = lax.bitwise_xor(me_col, d)
        return pltpu.make_async_remote_copy(
            leaving.at[(p, c) + piece], arriving.at[(p, me_col) + piece], sends.at[p, k, d], recvs.at[p, k, d],
            device_id=(me_row, c), device_id_type=MESH)

    def by_parity(p, odd, d):
        return passage(p, (odd,), odd, d)

    def by_depth(p, i, d):
        return passage(p, (slice(None), i), i, d)

    def whole(p, d):
        return passage(p, (), 0, d)

    group = pl.ds(me_row * cols, cols)
    row_copies = [
        pltpu.make_async_remote_copy(
            panels.at[group], panels.at[group], row_send.at[r], row_recv.at[r],
            device_id=peer(r, 0), device_id_type=MESH)
        for r in range(rows - 1, 0, -1)
    ]

    def pack(p, carry):
        @pl.when(p == 1)
        def _():
            for copy in panel_copies:
                copy.wait_recv()
            for copy in row_copies:
                copy.start()

        def columns(odd, inner):
            left = jnp.concatenate([made[p, pair, odd] for pair in range(listed // 2)], axis=1)
            for t in range(0, tiles, 2):
                width = min(2, tiles - t)
                right = jnp.concatenate(
                    [pick[t + k].reshape(listed * block_size, LANES) for k in range(width)], axis=1)
                value = jnp.dot(left, right, preferred_element_type=f32)
                for line in range(lines):
                    for g in range(2):
                        for k in range(width):
                            turned[t + k, pl.ds(g * 8 * lines + line, 8, stride=lines), :] = value[
                                line * 16 + g * 8 : line * 16 + g * 8 + 8, k * LANES : (k + 1) * LANES]
            for c in range(cols):
                for i in range(DEPTH):
                    row = (c * DEPTH + i) * lines
                    leaving[p, c, odd, i] = turned[:, row : row + lines, :].astype(bf16)

            @pl.when(p == 0)
            def _():
                for d in others[: cols // 2]:
                    by_parity(p, odd, d).start()

            return inner

        lax.fori_loop(0, 2, columns, 0)

        @pl.when(p == 0)
        def _():
            for d in others[cols // 2 :]:
                for odd in range(2):
                    by_parity(p, odd, d).start()

        @pl.when((p > 0) & (p < phases - 1))
        def _():
            for d in others:
                whole(p, d).start()

        @pl.when(p == phases - 1)
        def _():
            for i in range(DEPTH):
                for d in others:
                    by_depth(p, i, d).start()

        arriving[p, me_col] = leaving[p, me_col]
        return carry

    lax.fori_loop(0, phases, pack, 0)
    total_copies = share(totals.at[me], totals.at[me], 1, everyone, all_send, all_recv)
    for copy in list_copies:
        copy.wait_recv()
    mine = lists[...].reshape(cols * PLACES, LANES)
    if cols * PLACES < LANES:
        mine = jnp.concatenate([mine, jnp.full((LANES - cols * PLACES, LANES), 4 * LANES, i32)], axis=0)
    key = mine[:, 0:1]
    panel_of = mine[:, block_size : block_size + 1]
    places[...] = place(panel_of, LANES)[0]

    key_down = jnp.broadcast_to(key, square)
    key_across = jnp.broadcast_to(
        jnp.sum(jnp.where(down == across, key_down, 0), axis=0, keepdims=True), square)
    same_before = jnp.where((key_down == key_across) & (across < down), 1, 0)
    before = jnp.where(key_across < key_down, 1, 0) + same_before
    position = jnp.sum(before, axis=1, keepdims=True)
    repeats = jnp.minimum(jnp.sum(same_before, axis=1, keepdims=True), 1)
    at = position == across
    compact = down // PLACES * listed + down % PLACES
    table[0:1, :] = jnp.sum(jnp.where(at, compact, 0), axis=0, keepdims=True)
    table[1:2, :] = jnp.sum(jnp.where(at, repeats, 0), axis=0, keepdims=True)
    upto = jnp.sum(jnp.where(key_down <= across, 1, 0), axis=0, keepdims=True) - 1
    present = jnp.sum(jnp.where(key_down == across, 1, 0), axis=0, keepdims=True)
    table[2:3, :] = jnp.where(present > 0, upto, cols * listed)
    table[3:4, :] = jnp.sum(jnp.where(down == across, panel_of, 0), axis=0, keepdims=True)
    table[4:8, :] = jnp.zeros((4, LANES), i32)
    down_table = pltpu.make_async_copy(table, entry, moved)
    down_table.start()

    halves[cols * listed] = jnp.zeros((DEPTH, block_size, LANES), bf16)
    for a in range(2):
        tile[a * (side // 2) : (a + 1) * (side // 2), :] = jnp.zeros((side // 2, side), f32)
    down_table.wait()
    for copy in row_copies:
        copy.wait_recv()

    def gather(at_pair, carry):
        c, pair = at_pair // (listed // 2), at_pair % (listed // 2)
        for h in range(2):
            place = c * PLACES + pair * 2 + h
            spot = jnp.broadcast_to(places[pl.ds(place, 1), :][:, :block_size], (cap, block_size))
            chosen_rows = (spot == lax.broadcasted_iota(i32, (cap, block_size), 0).astype(f32)).astype(f32).astype(bf16)
            packed[c, pair, :, h * LANES : (h + 1) * LANES] = jnp.dot(
                chosen_rows, panels[entry[3, place]], preferred_element_type=f32).astype(bf16)
        return carry

    lax.fori_loop(0, cols * (listed // 2), gather, 0)

    def phase(p, first, count, arrived):
        def source(d, inner):
            c = lax.bitwise_xor(me_col, d)

            @pl.when(d > 0)
            def _():
                arrived(p, d)

            left = jnp.concatenate(
                [
                    jnp.concatenate([arriving[p, c, odd, first + i, t] for t in range(tiles)], axis=1)
                    for odd in range(2)
                    for i in range(count)
                ],
                axis=0,
            )
            for pair in range(listed // 2):
                value = jnp.dot(left, packed[c, pair], preferred_element_type=f32)
                for h in range(2):
                    for odd in range(2):
                        for i in range(count):
                            row = (odd * count + i) * lines
                            terms[c * listed + pair * 2 + h, i, pl.ds(odd, lines, stride=2), :] = value[
                                row : row + lines, h * LANES : (h + 1) * LANES]
            return inner

        lax.fori_loop(0, cols, source, 0)

        def segment(r, total):
            for k in range(4):
                at = r * 4 + k
                again = entry[1, at].astype(f32)
                total = terms[entry[0, at]][:count] + total * again
                halves[at, :count] = total.astype(bf16)
            return total

        lax.fori_loop(0, cols * listed // 4, segment, jnp.zeros((count, block_size, LANES), f32))

        batch = BATCH * DEPTH // count

        def products(s, inner):
            strip = []
            for a in range(MB):
                parts = []
                for k in range(batch):
                    cell = halves[entry[2, (s * batch + k) * MB + a]]
                    parts.extend(cell[i] for i in range(count))
                strip.append(jnp.concatenate(parts, axis=1))
            high = jnp.concatenate(strip[: MB // 2], axis=0)
            low = jnp.concatenate(strip[MB // 2 :], axis=0)
            half = side // 2
            for left, right, a, b in ((high, high, 0, 0), (high, low, 0, 1), (low, low, 1, 1)):
                tile[a * half : (a + 1) * half, b * half : (b + 1) * half] += lax.dot_general(
                    left, right, (((1,), (1,)), ((), ())), preferred_element_type=f32)
            return inner

        lax.fori_loop(0, slots // batch, products, 0)

    def early(p, carry):
        def arrived(p, d):
            @pl.when(p == 0)
            def _():
                for odd in range(2):
                    by_parity(p, odd, d).wait_recv()

            @pl.when(p > 0)
            def _():
                whole(p, d).wait_recv()

        phase(p, 0, DEPTH, arrived)
        return carry

    lax.fori_loop(0, phases - 1, early, 0)

    def late(i, carry):
        phase(phases - 1, i, 1, lambda p, d: by_depth(p, i, d).wait_recv())
        return carry

    lax.fori_loop(0, DEPTH, late, 0)
    half = side // 2
    tile[half:, :half] = tile[:half, half:].T

    scale = 1.0 / (slots * block_size * LANES)
    share = out_ref.shape[0]
    middle = cols // 2
    opposite = lax.bitwise_xor(me_col, middle)

    def rows_of(col):
        return pl.ds(pl.multiple_of(col * share, share), share)

    strips = [pl.ds(q * (side // 2), side // 2) for q in range(2)]
    near = {}
    for far_side, q in ((1, 0), (1, 1), (0, 0), (0, 1)):
        for d in range(1, middle):
            target = lax.bitwise_xor(me_col, d)
            near[far_side, q, d] = pltpu.make_async_remote_copy(
                tile.at[rows_of(lax.bitwise_xor(target, far_side * middle)), strips[q]],
                landed.at[far_side, d - 1, :, strips[q]],
                red_send.at[far_side, q, d], red_recv.at[far_side, q, d],
                device_id=(me_row, target), device_id_type=MESH)
            near[far_side, q, d].start()
    far = []
    for q in range(2):
        total = tile[rows_of(opposite), strips[q]]
        for d in range(1, middle):
            near[1, q, d].wait_recv()
            total = total + landed[1, d - 1, :, strips[q]]
        crossing[q] = total
        far.append(pltpu.make_async_remote_copy(
            crossing.at[q], crossed.at[q], red_send.at[0, q, 0], red_recv.at[0, q, 0],
            device_id=(me_row, opposite), device_id_type=MESH))
        far[-1].start()
    for copy in total_copies:
        copy.wait_recv()
    table[0:1, :] = jnp.max(totals[:, 0, :], axis=0, keepdims=True)
    verdict = pltpu.make_async_copy(table, entry, moved)
    verdict.start()
    for q in range(2):
        total = tile[rows_of(me_col), strips[q]]
        for d in range(1, middle):
            near[0, q, d].wait_recv()
            total = total + landed[0, d - 1, :, strips[q]]
        far[q].wait_recv()
        out_ref[:, strips[q]] = (total + crossed[q]) * scale
    verdict.wait()
    flag_ref[0] = (entry[0, 0] <= cap).astype(i32)
    copies = metric_copies + kept_copies + list_copies + panel_copies + row_copies + total_copies
    for copy in copies + list(near.values()) + far:
        copy.wait_send()

    def finish(p, carry):
        for d in others:
            whole(p, d).wait_send()
        return carry

    lax.fori_loop(1, phases - 1, finish, 0)
    for d in others:
        for k in range(2):
            by_parity(0, k, d).wait_send()
            by_depth(phases - 1, k, d).wait_send()


def fused(integrals, block_list, p_slot, metric, density_panel, pattern):
    rows, cols = lax.axis_size("row"), lax.axis_size("col")
    listed, block_size, flat = integrals.shape
    slots = metric.shape[0] * cols
    devices = rows * cols
    side = MB * block_size
    lines = flat // LANES
    phases = block_size // (cols * DEPTH)
    cap = -(-(listed * block_size * 5 // 6) // LANES) * LANES
    tiles = cap // LANES
    bf16, f32, i32 = jnp.bfloat16, jnp.float32, jnp.int32
    half = cols // 2
    dma = pltpu.SemaphoreType.DMA
    out, flag = pl.pallas_call(
        functools.partial(fused_kernel, rows, cols, cap),
        out_shape=(
            jax.ShapeDtypeStruct((side // cols, side), f32),
            jax.ShapeDtypeStruct((1,), i32),
        ),
        in_specs=[ANY] * 6,
        out_specs=(VMEM, SMEM),
        scratch_shapes=[
            pltpu.SMEM((3, listed), i32),
            pltpu.SMEM(p_slot.shape, i32),
            pltpu.VMEM((1, block_size), i32),
            pltpu.VMEM(density_panel.shape, bf16),
            pltpu.VMEM(metric.shape, bf16),
            dma((5,)),
            pltpu.VMEM((devices, 1, LANES), i32),
            pltpu.VMEM((devices, 1, LANES), i32),
            pltpu.VMEM((cols, PLACES, LANES), i32),
            pltpu.VMEM((slots, block_size, block_size), bf16),
            pltpu.VMEM((devices, block_size, LANES), bf16),
            pltpu.VMEM((listed, block_size, flat), bf16),
            pltpu.VMEM((phases, listed // 2, 2, lines * 16, LANES), bf16),
            pltpu.VMEM((tiles, listed, block_size, LANES), bf16),
            pltpu.VMEM((tiles, 16 * lines, LANES), f32),
            pltpu.VMEM((phases, cols, 2, DEPTH, tiles, lines, LANES), bf16),
            pltpu.VMEM((phases, cols, 2, DEPTH, tiles, lines, LANES), bf16),
            pltpu.VMEM((LANES, LANES), f32),
            pltpu.VMEM((8, LANES), i32),
            pltpu.SMEM((8, LANES), i32),
            pltpu.VMEM((cols, listed // 2, cap, 2 * LANES), bf16),
            pltpu.VMEM((cols * listed, DEPTH, block_size, LANES), f32),
            pltpu.VMEM((cols * listed + 1, DEPTH, block_size, LANES), bf16),
            pltpu.VMEM((side, side), f32),
            pltpu.VMEM((2, half - 1, side // cols, side), f32),
            pltpu.VMEM((2, side // cols, side // 2), f32),
            pltpu.VMEM((2, side // cols, side // 2), f32),
            dma((listed,)),
            dma((3, cols)),
            dma((3, cols)),
            dma((rows,)),
            dma((rows,)),
            dma((2, devices)),
            dma((2, devices)),
            dma((phases, 2, cols)),
            dma((phases, 2, cols)),
            dma((2, 2, half)),
            dma((2, 2, half)),
            dma,
        ],
        compiler_params=pltpu.CompilerParams(
            collective_id=3, has_side_effects=True, vmem_limit_bytes=63 * 2**20),
        name="fused",
    )(block_list.T, p_slot, pattern.reshape(1, -1), density_panel, metric, integrals)
    return out, flag


def on_device(integrals, block_list, p_slot, metric, density_panel, pattern):
    arguments = (integrals, block_list, p_slot, metric, density_panel, pattern)
    listed, block_size, flat = integrals.shape
    if not shapes_allow(
        lax.axis_size("row"), lax.axis_size("col"), listed, block_size, metric.shape[0],
        density_panel.shape[0], density_panel.shape[1], flat,
    ):
        return in_phases(*arguments)
    out, flag = fused(*arguments)
    return lax.cond(flag[0] > 0, lambda *_: out, in_phases, *arguments)


def solution(mesh):
    placed = (
        P(("row", "col"), None, None),
        P(("row", "col"), None),
        P(),
        P("col", None, None),
        P(("row", "col"), None),
        P(("row", "col")),
    )
    return jax.shard_map(
        on_device, mesh=mesh, in_specs=placed, out_specs=P(("row", "col"), None), check_vma=False
    )
```
